256 devices in a mesh: tm: 4 (over x), rows: 64 (over y, z, core).
Axes of the slice: x: 4, y: 4, z: 8, core: 2. Of those that a mesh axis runs over, the one named last changes fastest.
Arguments:
- latent: bfloat16 [4, 64, 160, 512], P('tm', 'rows'), may hold values from -350 to 350, as said below
- norm_gain: float32 [512], replicated, may hold values from 0.1 to 1.9
- norm_bias: float32 [512], replicated, may hold values from -4 to 4
- conv_weight: bfloat16 [3, 3, 3, 512, 512], P(None, None, None, 'rows', 'tm'), may hold values from -0.0546875 to 0.0546875
- cotangent: bfloat16 [4, 128, 320, 512], P('tm', 'rows'), may hold values from -180 to 180
Outputs:
- latent_grad: float32 [4, 64, 160, 512], P('tm', 'rows')
- gain_grad: float32 [512], replicated
- bias_grad: float32 [512], replicated
The draws below stay inside these ranges and needn't reach their ends.
Inputs may be any that keep to these rules, and one draw needn't show every extreme that they name: `latent`: features of the unit's input.
All inputs are finite; a program needn't handle non-finite values.
Results may differ from the reference program's by a relative error of at most 0.0003.
Values may be sent and summed in bfloat16 or wider, within the bound.
No kernel may reach another device: no remote copies, remote signals or barrier semaphores. Data moves between devices by JAX's collectives and lax.ppermute only.
A program may use at most 320 MiB of HBM per device.

```python
import math
import jax
import jax.numpy as jnp
from jax import lax

CH = 512
GROUPS = 32
COLS = 160
FRAMES = 4
LROWS = 64


def rising(count, factor):
    position = jnp.arange(count, dtype=jnp.float32) / max(count - 1, 1)
    return jnp.power(factor, position)


def draw_latent(key, part):
    key_parts = jax.random.split(key, 3)
    chan_scale = jnp.exp(jax.random.uniform(key_parts[0], (CH,), jnp.float32, math.log(0.5), math.log(5.0)))
    chan_offset = jax.random.uniform(key_parts[1], (CH,), jnp.float32, -1.0, 1.0)
    shape = (FRAMES, LROWS, COLS, CH)
    random_part = jnp.clip(jax.random.normal(key_parts[2], shape, jnp.float32), -4.0, 4.0)
    row_rise = rising(LROWS, 3.0)
    frame_rise = rising(FRAMES, 1.5)
    values = (random_part + chan_offset) * chan_scale * row_rise[None, :, None, None] * frame_rise[:, None, None, None]
    return values.astype(jnp.bfloat16)


def draw_cotangent(key, part):
    key_parts = jax.random.split(key, 3)
    chan_scale = jnp.exp(jax.random.uniform(key_parts[0], (CH,), jnp.float32, math.log(0.4), math.log(4.0)))
    chan_offset = jax.random.uniform(key_parts[1], (CH,), jnp.float32, -0.7, 0.7)
    shape = (FRAMES, 2 * LROWS, 2 * COLS, CH)
    random_part = jnp.clip(jax.random.normal(key_parts[2], shape, jnp.float32), -4.0, 4.0)
    row_rise = rising(2 * LROWS, 3.0)
    values = (random_part + chan_offset) * chan_scale * row_rise[None, :, None, None]
    return values.astype(jnp.bfloat16)


def level_of(key, shape, pieces, low, largest):
    def one(dim, shards_of):
        draws = jax.random.uniform(jax.random.fold_in(jax.random.fold_in(key, 6), dim), (shards_of,), jnp.float32, low / len(pieces), largest / len(pieces))
        return jnp.repeat(jnp.exp(draws), shape[dim] // shards_of).reshape((-1,) + (1,) * (len(shape) - dim - 1))

    gain = one(*pieces[0])
    for cut in pieces[1:]:
        gain = gain * one(*cut)
    return gain


def bell_draw(stream_key, extent, scale, bound, shards=(), held_as=jnp.bfloat16):
    level = level_of(stream_key, extent, shards, -0.22, 0.18) if shards else 1.0
    values = jax.random.normal(stream_key, extent, jnp.float32) * scale * level
    return jnp.minimum(jnp.maximum(values, -bound), bound).astype(held_as)


def setup_inputs(seed: int = 0) -> dict:
    key_list = jax.random.split(jax.random.key(seed), 6)
    latent = draw_latent(jax.random.fold_in(key_list[5], 71), 0)
    norm_gain = jnp.clip(1.0 + 0.18 * jax.random.normal(key_list[1], (CH,), jnp.float32), 0.1, 1.9)
    norm_bias = bell_draw(key_list[2], (CH,), 1.0, 4.0, (), jnp.float32)
    conv_weight = bell_draw(key_list[3], (3, 3, 3, CH, CH), (27 * CH) ** -0.5, 0.0546875, ((3, 64), (4, 4)))
    cotangent = draw_cotangent(jax.random.fold_in(key_list[5], 71), 0)
    return dict(latent=latent, norm_gain=norm_gain, norm_bias=norm_bias, conv_weight=conv_weight, cotangent=cotangent)


def tap_total(row_slabs, conv_weight, tap_pairs, frames_out, span_cols):
    running = None
    for offset, tap_index in tap_pairs:
        for row_tap in range(3):
            source = row_slabs[row_tap][offset:offset + frames_out].astype(jnp.float32)
            for col_tap in range(3):
                kernel = conv_weight[tap_index, row_tap, col_tap].astype(jnp.float32)
                product = lax.dot_general(source, kernel, (((3,), (1,)), ((), ())), precision=lax.Precision.HIGHEST, preferred_element_type=jnp.float32)
                piece = product[:, :, 2 - col_tap:2 - col_tap + span_cols, :]
                running = piece if running is None else running + piece
    return running

def pool_pairs(fine_grad):
    frames, fine_rows, span_cols, channels = fine_grad.shape
    return fine_grad.reshape(frames, fine_rows // 2, 2, span_cols // 2, 2, channels).sum(axis=(2, 4))

def reference(latent, norm_gain, norm_bias, conv_weight, cotangent):
    frames = cotangent.shape[0]
    fine_rows = cotangent.shape[1]
    span_cols = cotangent.shape[2]
    padded = jnp.pad(cotangent, ((0, 2), (1, 1), (1, 1), (0, 0)))
    row_slabs = [padded[:, 2 - row_tap:2 - row_tap + fine_rows] for row_tap in range(3)]
    main_part = tap_total(row_slabs, conv_weight, ((0, 2), (1, 1), (2, 0)), frames, span_cols)
    extra_part = tap_total(row_slabs, conv_weight, ((0, 1), (0, 0), (1, 0)), 1, span_cols)
    fine_grad = jnp.concatenate([main_part[:1] + extra_part, main_part[1:]], axis=0)
    up_grad = pool_pairs(fine_grad)
    channels = latent.shape[3]
    per_group = channels // GROUPS
    cell_count = latent.shape[0] * latent.shape[1] * latent.shape[2]
    features = latent.astype(jnp.float32)
    sum_x = lax.optimization_barrier(jnp.sum(features, axis=(0, 1, 2))).reshape(GROUPS, per_group).sum(axis=1)
    sum_sq = lax.optimization_barrier(jnp.sum(features * features, axis=(0, 1, 2))).reshape(GROUPS, per_group).sum(axis=1)
    group_mean = sum_x / (cell_count * per_group)
    group_var = sum_sq / (cell_count * per_group) - group_mean * group_mean
    inv_std = lax.rsqrt(group_var + 1e-06)
    mean_chan = jnp.repeat(group_mean, per_group)
    inv_chan = jnp.repeat(inv_std, per_group)
    normed = (features - mean_chan) * inv_chan
    pre = normed * norm_gain + norm_bias
    sigmoid_pre = jax.nn.sigmoid(pre)
    act_grad = up_grad * sigmoid_pre * (1.0 + pre * (1.0 - sigmoid_pre))
    sum_act = lax.optimization_barrier(jnp.sum(act_grad, axis=(0, 1, 2)))
    sum_scaled = lax.optimization_barrier(jnp.sum(act_grad * normed, axis=(0, 1, 2)))
    gain_grad = sum_scaled / cell_count
    bias_grad = sum_act / cell_count
    mean_q = (norm_gain * sum_act).reshape(GROUPS, per_group).sum(axis=1) / (cell_count * per_group)
    mean_qn = (norm_gain * sum_scaled).reshape(GROUPS, per_group).sum(axis=1) / (cell_count * per_group)
    latent_grad = inv_chan * (act_grad * norm_gain - jnp.repeat(mean_q, per_group) - normed * jnp.repeat(mean_qn, per_group))
    return (latent_grad, gain_grad, bias_grad)
```

```python
import functools

import jax
import jax.numpy as jnp
from jax import lax
from jax.experimental import pallas as pl
from jax.experimental.pallas import tpu as pltpu
from jax.sharding import PartitionSpec as P

GROUPS = 32
YS, ZS, CS = 4, 8, 2
ROWS = YS * ZS * CS
FRAMES = 4
TAPS = 9
UNITS = ((0, 1, 2, 3), (0, 1, 2), (0, 1))


def spot(y, z, c):
    return ((y % YS) * ZS + z % ZS) * CS + c


def rows_perm(move):
    pairs = []
    for y in range(YS):
        for z in range(ZS):
            for c in range(CS):
                pairs.append((spot(y, z, c), spot(*move(y, z, c))))
    return pairs


def send_y(value, step):
    return lax.ppermute(value, "rows", rows_perm(lambda y, z, c: (y + step, z, c)))


def send_z(value, step):
    return lax.ppermute(value, "rows", rows_perm(lambda y, z, c: (y, z + step, c)))


def swap_core(value):
    return lax.ppermute(value, "rows", rows_perm(lambda y, z, c: (y, z, 1 - c)))


def send_frames(value, step):
    return lax.ppermute(value, "tm", [(i, (i + step) % FRAMES) for i in range(FRAMES)])


def pool_kernel(cot0, cot1, cot2, cot3, low, high, out2, out1, out0, sums, pooled):
    cells = out2.shape[1] // FRAMES
    fine = 2 * cells
    place = lax.axis_index("tm")
    zero = jnp.zeros((8, 128), jnp.float32)
    for band in range(3):
        sums[band, 0:8] = zero
        sums[band, 8 + fine : 16 + fine] = zero
    for k, cot in enumerate((cot0, cot1, cot2, cot3)):
        frame = lax.rem(place + FRAMES - k, FRAMES)
        upper = cot[0].astype(jnp.float32)
        lower = cot[1].astype(jnp.float32)
        sums[0, 8 : 8 + fine] = lower + high[k].astype(jnp.float32)
        sums[1, 8 : 8 + fine] = upper + lower
        sums[2, 8 : 8 + fine] = low[k].astype(jnp.float32) + upper
        for band in range(3):
            at = sums.at[band]
            before = at[pl.ds(7, cells, stride=2), :]
            even = at[pl.ds(8, cells, stride=2), :]
            odd = at[pl.ds(9, cells, stride=2), :]
            after = at[pl.ds(10, cells, stride=2), :]
            pooled[frame, band * 3 + 0] = odd + after
            pooled[frame, band * 3 + 1] = even + odd
            pooled[frame, band * 3 + 2] = before + even
    for tap in range(TAPS):
        lanes = slice(tap * 128, tap * 128 + 128)

        def put(out, unit, value):
            head = value.astype(jnp.bfloat16)
            tail = (value - head.astype(jnp.float32)).astype(jnp.bfloat16)
            out[0, unit * cells : (unit + 1) * cells, lanes] = head
            out[1, unit * cells : (unit + 1) * cells, lanes] = tail

        p0, p1, p2, p3 = (pooled[t, tap] for t in range(FRAMES))
        put(out2, 0, p0)
        put(out2, 1, p1)
        put(out2, 2, p2)
        put(out2, 3, p3)
        p01 = p0 + p1
        put(out1, 0, p01)
        put(out1, 1, p2)
        put(out1, 2, p3)
        put(out0, 0, p01 + p2)
        put(out0, 1, p3)


def pool(cots, low, high):
    cells = cots[0].shape[1] // 2
    shapes = [
        jax.ShapeDtypeStruct((2, len(units) * cells, TAPS * 128), jnp.bfloat16) for units in UNITS
    ]
    return pl.pallas_call(
        pool_kernel,
        out_shape=shapes,
        in_specs=[pl.BlockSpec(memory_space=pltpu.VMEM)] * 6,
        out_specs=[pl.BlockSpec(memory_space=pltpu.VMEM)] * 3,
        scratch_shapes=[
            pltpu.VMEM((3, 2 * cells + 16, 128), jnp.float32),
            pltpu.VMEM((FRAMES, TAPS, cells, 128), jnp.float32),
        ],
        compiler_params=pltpu.CompilerParams(vmem_limit_bytes=40 << 20),
        cost_estimate=pl.CostEstimate(flops=20_000_000, bytes_accessed=9_000_000, transcendentals=0),
    )(*cots, low, high)


def product_kernel(z_steps, *refs):
    pieces = refs[: 2 * len(z_steps)]
    left2, left1, left0, out, weights, sems = refs[2 * len(z_steps) :]
    at = lax.axis_index("rows")
    y, z, c = at // (ZS * CS), lax.rem(at // CS, ZS), lax.rem(at, CS)
    copies = []
    for side in range(2):
        core = c if side == 0 else 1 - c
        for index, (step, first) in enumerate(z_steps):
            piece = pieces[side * len(z_steps) + index]
            source_z = lax.rem(z + ZS - step, ZS)
            for j in range(piece.shape[0]):
                source_y = lax.rem(y + YS - (first + j), YS)
                row = pl.multiple_of(source_y * (ZS * CS * 8) + source_z * (CS * 8) + core * 8, 8)
                copies.append(
                    pltpu.make_async_copy(
                        piece.at[j, 0 : 3 * TAPS],
                        weights.at[:, pl.ds(row, 8), :],
                        sems.at[len(copies)],
                    )
                )
    for copy in copies:
        copy.start()
    for copy in copies:
        copy.wait()
    for n in range(out.shape[1] // 256):
        cols = slice(n * 256, n * 256 + 256)
        for tap, left in ((2, left2), (1, left1), (0, left0)):
            right = jnp.concatenate(
                [weights[tap * TAPS + t, cols, :] for t in range(TAPS)], axis=1
            )
            total = None
            for half in range(2):
                part = lax.dot_general(
                    left[half], right, (((1,), (1,)), ((), ())), preferred_element_type=jnp.float32
                )
                total = part if total is None else total + part
            if tap == 2:
                out[:, cols] = total
            else:
                out[0 : total.shape[0], cols] += total


def product(pieces, z_steps, lefts, channels):
    rows = lefts[0].shape[1]
    count = 2 * sum(piece.shape[0] for piece in pieces[: len(z_steps)])
    return pl.pallas_call(
        functools.partial(product_kernel, z_steps),
        out_shape=jax.ShapeDtypeStruct((rows, channels), jnp.float32),
        in_specs=[pl.BlockSpec(memory_space=pl.ANY)] * len(pieces)
        + [pl.BlockSpec(memory_space=pltpu.VMEM)] * 3,
        out_specs=pl.BlockSpec(memory_space=pltpu.VMEM),
        scratch_shapes=[
            pltpu.VMEM((3 * TAPS, channels, 128), jnp.bfloat16),
            pltpu.SemaphoreType.DMA((count,)),
        ],
        compiler_params=pltpu.CompilerParams(vmem_limit_bytes=40 << 20),
        cost_estimate=pl.CostEstimate(
            flops=3_400_000_000, bytes_accessed=11_000_000, transcendentals=0
        ),
    )(*pieces, *lefts)


def three_parts(value):
    head = lax.reduce_precision(value, 8, 7)
    rest = value - head
    middle = lax.reduce_precision(rest, 8, 7)
    return [part.astype(jnp.bfloat16) for part in (head, middle, rest - middle)]


def on_device(latent, norm_gain, norm_bias, conv_weight, cotangent):
    place = lax.axis_index("tm")
    cells, channels = latent.shape[2], latent.shape[3]
    fine_cols = cotangent.shape[2]
    per_group = channels // GROUPS
    cell_count = FRAMES * ROWS * cells

    own = latent[0, 0].astype(jnp.float32)
    stats = jnp.stack([jnp.sum(own, axis=0), jnp.sum(own * own, axis=0)])
    parts = jnp.stack([part.reshape(8, 128) for part in three_parts(stats)])
    message = jnp.concatenate([conv_weight.reshape(3 * TAPS, 8, 128), parts], axis=0)
    block = jnp.stack([message] + [send_y(message, step) for step in range(1, YS)])
    forth, back = block, block
    pieces, z_steps = [block], [(0, 0)]
    for step in range(1, ZS // 2):
        forth, back = send_z(forth, 1), send_z(back, -1)
        pieces += [forth, back]
        z_steps += [(step, 0), (-step, 0)]
    half = YS // 2
    pieces += [send_z(forth[:half], 1), send_z(back[half:], -1)]
    z_steps += [(ZS // 2, 0), (ZS // 2, half)]
    pieces = pieces + [swap_core(piece) for piece in pieces]

    latents = [latent[0, 0]] + [send_frames(latent[0, 0], step) for step in range(1, FRAMES)]
    split = cotangent[0].reshape(2, fine_cols, FRAMES, 128).transpose(2, 0, 1, 3)
    cots = []
    for step in range(FRAMES):
        chunk = lax.dynamic_index_in_dim(split, lax.rem(place + step, FRAMES), 0, keepdims=False)
        cots.append(chunk if step == 0 else send_frames(chunk, step))
    low = lax.ppermute(
        jnp.stack([cot[1] for cot in cots]), "rows", [(i, i + 1) for i in range(ROWS - 1)]
    )
    high = lax.ppermute(
        jnp.stack([cot[0] for cot in cots]), "rows", [(i + 1, i) for i in range(ROWS - 1)]
    )
    lefts = pool(cots, low, high)
    partial = product(pieces, tuple(z_steps), lefts, channels).reshape(FRAMES, cells, channels)

    gathered = sum(
        jnp.sum(piece[:, 3 * TAPS :].astype(jnp.float32), axis=(0, 1)) for piece in pieces
    ).reshape(2, channels)
    total = gathered + sum(send_frames(gathered, step) for step in range(1, FRAMES))
    group = total.reshape(2, GROUPS, per_group).sum(axis=2) / (cell_count * per_group)
    group_mean = group[0]
    group_var = group[1] - group_mean * group_mean
    inv_std = lax.rsqrt(group_var + 1e-06)
    mean_chan = jnp.repeat(group_mean, per_group)
    inv_chan = jnp.repeat(inv_std, per_group)

    def slope(features):
        normed = (features.astype(jnp.float32) - mean_chan) * inv_chan
        pre = normed * norm_gain + norm_bias
        sigmoid_pre = jax.nn.sigmoid(pre)
        return normed, sigmoid_pre * (1.0 + pre * (1.0 - sigmoid_pre))

    here = []
    for step in range(FRAMES):
        frame = lax.rem(place + FRAMES - step, FRAMES)
        here.append(lax.dynamic_index_in_dim(partial, frame, 0, keepdims=False))
    sum_act = jnp.zeros((channels,), jnp.float32)
    sum_scaled = jnp.zeros((channels,), jnp.float32)
    for step in range(FRAMES):
        normed, gate = slope(latents[step])
        act = here[step] * gate
        sum_act = sum_act + jnp.sum(act, axis=0)
        sum_scaled = sum_scaled + jnp.sum(act * normed, axis=0)
    up_grad = here[0] + sum(
        send_frames(here[FRAMES - step], step) for step in range(1, FRAMES)
    )
    sums = jnp.stack([sum_act, sum_scaled]).reshape(1, 8, 128)
    sums = lax.all_to_all(
        jnp.broadcast_to(sums, (ROWS, 8, 128)), "rows", 0, 0, tiled=True
    ).sum(axis=0)
    sums = sums + sum(send_frames(sums, step) for step in range(1, FRAMES))
    sum_act, sum_scaled = sums.reshape(2, channels)

    gain_grad = sum_scaled / cell_count
    bias_grad = sum_act / cell_count
    scale = cell_count * per_group
    mean_q = (norm_gain * sum_act).reshape(GROUPS, per_group).sum(axis=1) / scale
    mean_qn = (norm_gain * sum_scaled).reshape(GROUPS, per_group).sum(axis=1) / scale
    normed, gate = slope(latents[0])
    latent_grad = inv_chan * (
        up_grad * gate * norm_gain
        - jnp.repeat(mean_q, per_group)
        - normed * jnp.repeat(mean_qn, per_group)
    )
    return (latent_grad.reshape(1, 1, cells, channels), gain_grad, bias_grad)


def solution(mesh):
    placed = (
        P("tm", "rows", None, None),
        P(),
        P(),
        P(None, None, None, "rows", "tm"),
        P("tm", "rows", None, None),
    )
    return jax.shard_map(
        on_device,
        mesh=mesh,
        in_specs=placed,
        out_specs=(P("tm", "rows", None, None), P(), P()),
        check_vma=False,
    )
```

```python
import functools

import jax
import jax.numpy as jnp
from jax import lax
from jax.experimental import pallas as pl
from jax.experimental.pallas import tpu as pltpu
from jax.sharding import Mesh
from jax.sharding import PartitionSpec as P

GROUPS = 32
XS, YS, ZS, CS = 4, 4, 8, 2
ROWS = YS * ZS * CS
FRAMES = XS
SIZES = {"x": XS, "y": YS, "z": ZS, "c": CS}
ROW_AXES = ("y", "z", "c")
TAPS = 9
PLANES = 3 * TAPS
UNITS = ((0, 1, 2, 3), (0, 1, 2), (0, 1))
VMEM = pl.BlockSpec(memory_space=pltpu.VMEM)


def send(value, axis, step):
    size = SIZES[axis]
    return lax.ppermute(value, axis, [(i, (i + step) % size) for i in range(size)])


def pool_kernel(msg0, msg1, msg2, msg3, low, high, out2, out1, out0, sums, pooled):
    cells = out2.shape[1] // FRAMES
    fine = 2 * cells
    place = lax.axis_index("x")
    zero = jnp.zeros((8, 128), jnp.float32)
    for band in range(3):
        sums[band, 0:8] = zero
        sums[band, 8 + fine : 16 + fine] = zero
    for k, msg in enumerate((msg0, msg1, msg2, msg3)):
        frame = lax.rem(place + FRAMES - k, FRAMES)
        upper = msg[0:fine].astype(jnp.float32)
        lower = msg[fine : 2 * fine].astype(jnp.float32)
        sums[0, 8 : 8 + fine] = lower + high[k].astype(jnp.float32)
        sums[1, 8 : 8 + fine] = upper + lower
        sums[2, 8 : 8 + fine] = low[k].astype(jnp.float32) + upper
        for band in range(3):
            at = sums.at[band]
            before = at[pl.ds(7, cells, stride=2), :]
            even = at[pl.ds(8, cells, stride=2), :]
            odd = at[pl.ds(9, cells, stride=2), :]
            after = at[pl.ds(10, cells, stride=2), :]
            pooled[frame, band * 3 + 0] = odd + after
            pooled[frame, band * 3 + 1] = even + odd
            pooled[frame, band * 3 + 2] = before + even
    for tap in range(TAPS):
        lanes = slice(tap * 128, tap * 128 + 128)

        def put(out, unit, value):
            head = value.astype(jnp.bfloat16)
            tail = (value - head.astype(jnp.float32)).astype(jnp.bfloat16)
            out[0, unit * cells : (unit + 1) * cells, lanes] = head
            out[1, unit * cells : (unit + 1) * cells, lanes] = tail

        p0, p1, p2, p3 = (pooled[t, tap] for t in range(FRAMES))
        put(out2, 0, p0)
        put(out2, 1, p1)
        put(out2, 2, p2)
        put(out2, 3, p3)
        p01 = p0 + p1
        put(out1, 0, p01)
        put(out1, 1, p2)
        put(out1, 2, p3)
        put(out0, 0, p01 + p2)
        put(out0, 1, p3)


def pool(msgs, low, high):
    cells = low.shape[1] // 2
    shapes = [
        jax.ShapeDtypeStruct((2, len(units) * cells, TAPS * 128), jnp.bfloat16) for units in UNITS
    ]
    return pl.pallas_call(
        pool_kernel,
        out_shape=shapes,
        in_specs=[VMEM] * 6,
        out_specs=[VMEM] * 3,
        scratch_shapes=[
            pltpu.VMEM((3, 2 * cells + 16, 128), jnp.float32),
            pltpu.VMEM((FRAMES, TAPS, cells, 128), jnp.float32),
        ],
        compiler_params=pltpu.CompilerParams(vmem_limit_bytes=12 << 20),
        cost_estimate=pl.CostEstimate(flops=20_000_000, bytes_accessed=9_000_000, transcendentals=0),
    )(*msgs, low, high)


def product_kernel(*refs):
    pieces = refs[: CS * YS]
    left2, left1, left0 = refs[CS * YS : CS * YS + 3]
    outs = refs[CS * YS + 3 : CS * YS + 7]
    weights, acc, sems = refs[CS * YS + 7 :]
    y, c = lax.axis_index("y"), lax.axis_index("c")
    cells = outs[0].shape[0]
    copies = []
    for side in range(CS):
        core = c if side == 0 else 1 - c
        for step in range(YS):
            piece = pieces[side * YS + step]
            source_y = lax.rem(y + YS - step, YS)
            for z in range(ZS):
                row = pl.multiple_of(source_y * (ZS * CS * 8) + z * (CS * 8) + core * 8, 8)
                copies.append(
                    pltpu.make_async_copy(
                        piece.at[z, 0:PLANES],
                        weights.at[:, pl.ds(row, 8), :],
                        sems.at[len(copies)],
                    )
                )
    for copy in copies:
        copy.start()
    for copy in copies:
        copy.wait()
    for n in range(acc.shape[1] // 256):
        cols = slice(n * 256, n * 256 + 256)
        for tap, left in ((2, left2), (1, left1), (0, left0)):
            right = jnp.concatenate(
                [weights[tap * TAPS + t, cols, :] for t in range(TAPS)], axis=1
            )
            total = None
            for half in range(2):
                part = lax.dot_general(
                    left[half], right, (((1,), (1,)), ((), ())), preferred_element_type=jnp.float32
                )
                total = part if total is None else total + part
            if tap == 2:
                acc[:, cols] = total
            else:
                acc[0 : total.shape[0], cols] += total
    place = lax.axis_index("x")
    for k, out in enumerate(outs):
        frame = lax.rem(place + FRAMES - k, FRAMES)
        out[...] = acc[pl.ds(pl.multiple_of(frame * cells, 8), cells), :]


def product(pieces, lefts, channels):
    cells = lefts[0].shape[1] // FRAMES
    return pl.pallas_call(
        product_kernel,
        out_shape=[jax.ShapeDtypeStruct((cells, channels), jnp.float32)] * FRAMES,
        in_specs=[pl.BlockSpec(memory_space=pl.ANY)] * len(pieces) + [VMEM] * 3,
        out_specs=[VMEM] * FRAMES,
        scratch_shapes=[
            pltpu.VMEM((PLANES, channels, 128), jnp.bfloat16),
            pltpu.VMEM((FRAMES * cells, channels), jnp.float32),
            pltpu.SemaphoreType.DMA((CS * YS * ZS,)),
        ],
        compiler_params=pltpu.CompilerParams(vmem_limit_bytes=14 << 20),
        cost_estimate=pl.CostEstimate(
            flops=3_400_000_000, bytes_accessed=11_000_000, transcendentals=0
        ),
    )(*pieces, *lefts)


def sums_kernel(part0, part1, part2, part3, msg0, msg1, msg2, msg3, chan, out):
    cells, channels = part0.shape
    offset = msg0.shape[0] - 4 * cells
    for q in range(channels // 128):
        lanes = slice(q * 128, q * 128 + 128)
        mean, inv, gain, bias = (chan[r : r + 1, lanes] for r in range(4))
        first = jnp.zeros((8, 128), jnp.float32)
        second = jnp.zeros((8, 128), jnp.float32)
        for part, msg in ((part0, msg0), (part1, msg1), (part2, msg2), (part3, msg3)):
            start = offset + q * cells
            features = msg[start : start + cells].astype(jnp.float32)
            normed = (features - mean) * inv
            pre = normed * gain + bias
            sigmoid_pre = 1.0 / (1.0 + jnp.exp(-pre))
            act = part[:, lanes] * (sigmoid_pre * (1.0 + pre * (1.0 - sigmoid_pre)))
            first = first + act.reshape(cells // 8, 8, 128).sum(axis=0)
            second = second + (act * normed).reshape(cells // 8, 8, 128).sum(axis=0)
        out[q : q + 1] = jnp.sum(first, axis=0, keepdims=True)
        out[4 + q : 5 + q] = jnp.sum(second, axis=0, keepdims=True)


def partial_sums(parts, msgs, chan):
    return pl.pallas_call(
        sums_kernel,
        out_shape=jax.ShapeDtypeStruct((8, 128), jnp.float32),
        in_specs=[VMEM] * 9,
        out_specs=VMEM,
        compiler_params=pltpu.CompilerParams(vmem_limit_bytes=6 << 20),
        cost_estimate=pl.CostEstimate(
            flops=6_000_000, bytes_accessed=2_600_000, transcendentals=330_000
        ),
    )(*parts, *msgs, chan)


def three_parts(value):
    head = lax.reduce_precision(value, 8, 7)
    rest = value - head
    middle = lax.reduce_precision(rest, 8, 7)
    return [part.astype(jnp.bfloat16) for part in (head, middle, rest - middle)]


def on_device(latent, norm_gain, norm_bias, conv_weight, cotangent):
    place = lax.axis_index("x")
    cells, channels = latent.shape[2], latent.shape[3]
    fine_cols = cotangent.shape[2]
    per_group = channels // GROUPS
    cell_count = FRAMES * ROWS * cells

    split = cotangent[0].reshape(2 * fine_cols, FRAMES, 128).transpose(1, 0, 2)
    shared = latent[0, 0].reshape(cells, 4, 128).transpose(1, 0, 2).reshape(4 * cells, 128)
    msgs = []
    for step in range(FRAMES):
        chunk = lax.dynamic_index_in_dim(split, lax.rem(place + step, FRAMES), 0, keepdims=False)
        msgs.append(jnp.concatenate([chunk, shared], axis=0))
    msgs = [msg if step == 0 else send(msg, "x", step) for step, msg in enumerate(msgs)]

    own = latent[0, 0].astype(jnp.float32)
    stats = jnp.stack([jnp.sum(own, axis=0), jnp.sum(own * own, axis=0)])
    parts = jnp.stack([part.reshape(8, 128) for part in three_parts(stats)])
    message = jnp.concatenate([conv_weight.reshape(PLANES, 8, 128), parts], axis=0)
    block = lax.all_to_all(
        jnp.broadcast_to(message[None], (ZS,) + message.shape), "z", 0, 0, tiled=True
    )
    pieces = [block] + [send(block, "y", step) for step in range(1, YS)]
    pieces = pieces + [send(piece, "c", 1) for piece in pieces]

    low = lax.ppermute(
        jnp.stack([msg[fine_cols : 2 * fine_cols] for msg in msgs]),
        ROW_AXES,
        [(i, i + 1) for i in range(ROWS - 1)],
    )
    high = lax.ppermute(
        jnp.stack([msg[:fine_cols] for msg in msgs]),
        ROW_AXES,
        [(i + 1, i) for i in range(ROWS - 1)],
    )
    lefts = pool(msgs, low, high)
    partial = product(pieces, lefts, channels)

    gathered = sum(
        jnp.sum(piece[:, PLANES:].astype(jnp.float32), axis=(0, 1)) for piece in pieces
    )
    total = gathered + sum(send(gathered, "x", step) for step in range(1, FRAMES))
    group = total.reshape(2, GROUPS, per_group).sum(axis=2) / (cell_count * per_group)
    group_mean = group[0]
    group_var = group[1] - group_mean * group_mean
    inv_std = lax.rsqrt(group_var + 1e-06)
    mean_chan = jnp.repeat(group_mean, per_group)
    inv_chan = jnp.repeat(inv_std, per_group)

    chan = jnp.stack([mean_chan, inv_chan, norm_gain, norm_bias])
    sums = partial_sums(partial, msgs, chan)
    sums = sums + sum(send(sums, "x", step) for step in range(1, FRAMES))
    up_grad = partial[0] + sum(
        send(partial[FRAMES - step], "x", step) for step in range(1, FRAMES)
    )
    sums = lax.all_to_all(
        jnp.broadcast_to(sums[None], (ROWS, 8, 128)), ROW_AXES, 0, 0, tiled=True
    ).sum(axis=0)
    sum_act, sum_scaled = sums.reshape(2, channels)

    gain_grad = sum_scaled / cell_count
    bias_grad = sum_act / cell_count
    scale = cell_count * per_group
    mean_q = (norm_gain * sum_act).reshape(GROUPS, per_group).sum(axis=1) / scale
    mean_qn = (norm_gain * sum_scaled).reshape(GROUPS, per_group).sum(axis=1) / scale
    normed = (own - mean_chan) * inv_chan
    pre = normed * norm_gain + norm_bias
    sigmoid_pre = jax.nn.sigmoid(pre)
    act_grad = up_grad * sigmoid_pre * (1.0 + pre * (1.0 - sigmoid_pre))
    latent_grad = inv_chan * (
        act_grad * norm_gain
        - jnp.repeat(mean_q, per_group)
        - normed * jnp.repeat(mean_qn, per_group)
    )
    return (latent_grad.reshape(1, 1, cells, channels), gain_grad, bias_grad)


def solution(mesh):
    fine = Mesh(mesh.devices.reshape(XS, YS, ZS, CS), ("x", "y", "z", "c"))
    image = P("x", ROW_AXES, None, None)
    return jax.shard_map(
        on_device,
        mesh=fine,
        in_specs=(image, P(), P(), P(None, None, None, ROW_AXES, "x"), image),
        out_specs=(image, P(), P()),
        check_vma=False,
    )
```

```python
import functools

import jax
import jax.numpy as jnp
from jax import lax
from jax.experimental import pallas as pl
from jax.experimental.pallas import tpu as pltpu
from jax.sharding import Mesh
from jax.sharding import PartitionSpec as P

GROUPS = 32
XS, YS, ZS, CS = 4, 4, 8, 2
ROWS = YS * ZS * CS
FRAMES = XS
SIZES = {"x": XS, "y": YS, "z": ZS, "c": CS}
ROW_AXES = ("y", "z", "c")
TAPS = 9
PLANES = 3 * TAPS
UNITS = ((0, 1, 2, 3), (0, 1, 2), (0, 1))
VMEM = pl.BlockSpec(memory_space=pltpu.VMEM)


def send(value, axis, step):
    size = SIZES[axis]
    return lax.ppermute(value, axis, [(i, (i + step) % size) for i in range(size)])


def pool_kernel(msg0, msg1, msg2, msg3, low, high, out2, out1, out0, sums, pooled):
    cells = out2.shape[1] // FRAMES
    fine = 2 * cells
    place = lax.axis_index("x")
    zero = jnp.zeros((8, 128), jnp.float32)
    for band in range(3):
        sums[band, 0:8] = zero
        sums[band, 8 + fine : 16 + fine] = zero
    for k, msg in enumerate((msg0, msg1, msg2, msg3)):
        frame = lax.rem(place + FRAMES - k, FRAMES)
        upper = msg[0].astype(jnp.float32)
        lower = msg[1].astype(jnp.float32)
        sums[0, 8 : 8 + fine] = lower + high[k].astype(jnp.float32)
        sums[1, 8 : 8 + fine] = upper + lower
        sums[2, 8 : 8 + fine] = low[k].astype(jnp.float32) + upper
        for band in range(3):
            at = sums.at[band]
            before = at[pl.ds(7, cells, stride=2), :]
            even = at[pl.ds(8, cells, stride=2), :]
            odd = at[pl.ds(9, cells, stride=2), :]
            after = at[pl.ds(10, cells, stride=2), :]
            pooled[frame, band * 3 + 0] = odd + after
            pooled[frame, band * 3 + 1] = even + odd
            pooled[frame, band * 3 + 2] = before + even
    for tap in range(TAPS):
        lanes = slice(tap * 128, tap * 128 + 128)

        def put(out, unit, value):
            head = value.astype(jnp.bfloat16)
            tail = (value - head.astype(jnp.float32)).astype(jnp.bfloat16)
            out[0, unit * cells : (unit + 1) * cells, lanes] = head
            out[1, unit * cells : (unit + 1) * cells, lanes] = tail

        p0, p1, p2, p3 = (pooled[t, tap] for t in range(FRAMES))
        put(out2, 0, p0)
        put(out2, 1, p1)
        put(out2, 2, p2)
        put(out2, 3, p3)
        p01 = p0 + p1
        put(out1, 0, p01)
        put(out1, 1, p2)
        put(out1, 2, p3)
        put(out0, 0, p01 + p2)
        put(out0, 1, p3)


def pool(msgs, low, high):
    cells = low.shape[1] // 2
    shapes = [
        jax.ShapeDtypeStruct((2, len(units) * cells, TAPS * 128), jnp.bfloat16) for units in UNITS
    ]
    return pl.pallas_call(
        pool_kernel,
        out_shape=shapes,
        in_specs=[VMEM] * 6,
        out_specs=[VMEM] * 3,
        scratch_shapes=[
            pltpu.VMEM((3, 2 * cells + 16, 128), jnp.float32),
            pltpu.VMEM((FRAMES, TAPS, cells, 128), jnp.float32),
        ],
        compiler_params=pltpu.CompilerParams(vmem_limit_bytes=12 << 20),
        cost_estimate=pl.CostEstimate(flops=20_000_000, bytes_accessed=9_000_000, transcendentals=0),
    )(*msgs, low, high)


def split_kernel(cot, out0, out1, out2, out3, sems):
    place = lax.axis_index("x")
    copies = []
    for k, out in enumerate((out0, out1, out2, out3)):
        first = pl.multiple_of(lax.rem(place + k, FRAMES) * 128, 128)
        copies.append(pltpu.make_async_copy(cot.at[0, :, :, pl.ds(first, 128)], out, sems.at[k]))
    for copy in copies:
        copy.start()
    for copy in copies:
        copy.wait()


def split(cotangent):
    shape = jax.ShapeDtypeStruct(cotangent.shape[1:3] + (128,), cotangent.dtype)
    return pl.pallas_call(
        split_kernel,
        out_shape=[shape] * FRAMES,
        in_specs=[pl.BlockSpec(memory_space=pl.ANY)],
        out_specs=[VMEM] * FRAMES,
        scratch_shapes=[pltpu.SemaphoreType.DMA((FRAMES,))],
        compiler_params=pltpu.CompilerParams(vmem_limit_bytes=2 << 20),
        cost_estimate=pl.CostEstimate(flops=0, bytes_accessed=1_300_000, transcendentals=0),
    )(cotangent)


def message_kernel(latent, weight, out, stats):
    channels = latent.shape[1]
    for q in range(channels // 128):
        values = latent[:, q * 128 : q * 128 + 128].astype(jnp.float32)
        stats[q : q + 1] = jnp.sum(values, axis=0, keepdims=True)
        stats[4 + q : 5 + q] = jnp.sum(values * values, axis=0, keepdims=True)
    total = stats[...]
    head = total.astype(jnp.bfloat16)
    rest = total - head.astype(jnp.float32)
    middle = rest.astype(jnp.bfloat16)
    last = (rest - middle.astype(jnp.float32)).astype(jnp.bfloat16)
    for z in range(ZS):
        out[z, 0:PLANES] = weight[...]
        out[z, PLANES] = head
        out[z, PLANES + 1] = middle
        out[z, PLANES + 2] = last


def message(latent, weight):
    return pl.pallas_call(
        message_kernel,
        out_shape=jax.ShapeDtypeStruct((ZS, PLANES + 3, 8, 128), jnp.bfloat16),
        in_specs=[VMEM] * 2,
        out_specs=VMEM,
        scratch_shapes=[pltpu.VMEM((8, 128), jnp.float32)],
        compiler_params=pltpu.CompilerParams(vmem_limit_bytes=3 << 20),
        cost_estimate=pl.CostEstimate(flops=250_000, bytes_accessed=720_000, transcendentals=0),
    )(latent, weight)


def rims_kernel(msg0, msg1, msg2, msg3, first, last):
    for k, msg in enumerate((msg0, msg1, msg2, msg3)):
        first[k] = msg[0]
        last[k] = msg[1]


def rims(msgs):
    shape = jax.ShapeDtypeStruct((FRAMES,) + msgs[0].shape[1:], jnp.bfloat16)
    return pl.pallas_call(
        rims_kernel,
        out_shape=[shape] * 2,
        in_specs=[VMEM] * FRAMES,
        out_specs=[VMEM] * 2,
        compiler_params=pltpu.CompilerParams(vmem_limit_bytes=3 << 20),
        cost_estimate=pl.CostEstimate(flops=0, bytes_accessed=1_300_000, transcendentals=0),
    )(*msgs)


def product_kernel(steps, aliased, *refs):
    count = CS * len(steps)
    pieces = refs[:count]
    left2, left1, left0 = refs[count : count + 3]
    skip = count + 3 + (FRAMES if aliased else 0)
    outs = refs[skip : skip + FRAMES]
    weights, acc, sems = refs[skip + FRAMES :]
    y, c = lax.axis_index("y"), lax.axis_index("c")
    cells = outs[0].shape[1]
    copies = []
    for index, step in enumerate(steps):
        for side in range(CS):
            core = c if side == 0 else 1 - c
            piece = pieces[index * CS + side]
            for z in range(ZS):
                row = pl.multiple_of(index * 128 + z * (CS * 8) + core * 8, 8)
                copies.append(
                    pltpu.make_async_copy(
                        piece.at[z, 0:PLANES],
                        weights.at[:, pl.ds(row, 8), :],
                        sems.at[len(copies)],
                    )
                )
    for copy in copies:
        copy.start()
    for copy in copies:
        copy.wait()
    for tap, left in ((2, left2), (1, left1), (0, left0)):
        right = jnp.concatenate([weights[tap * TAPS + t] for t in range(TAPS)], axis=1)
        total = None
        for half in range(2):
            part = lax.dot_general(
                left[half], right, (((1,), (1,)), ((), ())), preferred_element_type=jnp.float32
            )
            total = part if total is None else total + part
        if tap == 2:
            acc[...] = total
        else:
            acc[0 : total.shape[0]] += total
    place = lax.axis_index("x")
    for index, step in enumerate(steps):
        source_y = lax.rem(y + YS - step, YS)
        lanes = slice(index * 128, index * 128 + 128)
        for k, out in enumerate(outs):
            frame = lax.rem(place + FRAMES - k, FRAMES)
            out[source_y] = acc[pl.ds(pl.multiple_of(frame * cells, 8), cells), lanes]


def product(pieces, steps, lefts, before):
    cells = lefts[0].shape[1] // FRAMES
    aliased = before is not None
    inputs = [*pieces, *lefts, *(before if aliased else [])]
    return pl.pallas_call(
        functools.partial(product_kernel, steps, aliased),
        out_shape=[jax.ShapeDtypeStruct((YS, cells, 128), jnp.float32)] * FRAMES,
        in_specs=[pl.BlockSpec(memory_space=pl.ANY)] * len(pieces)
        + [VMEM] * (len(inputs) - len(pieces)),
        out_specs=[VMEM] * FRAMES,
        scratch_shapes=[
            pltpu.VMEM((PLANES, len(steps) * 128, 128), jnp.bfloat16),
            pltpu.VMEM((FRAMES * cells, len(steps) * 128), jnp.float32),
            pltpu.SemaphoreType.DMA((CS * ZS * len(steps),)),
        ],
        input_output_aliases={len(pieces) + 3 + k: k for k in range(FRAMES)} if aliased else {},
        compiler_params=pltpu.CompilerParams(vmem_limit_bytes=12 << 20),
        cost_estimate=pl.CostEstimate(
            flops=1_700_000_000, bytes_accessed=9_000_000, transcendentals=0
        ),
    )(*inputs)


def slope(features, chan, lanes):
    mean, inv, gain, bias = (chan[r : r + 1, lanes] for r in range(4))
    normed = (features.astype(jnp.float32) - mean) * inv
    pre = normed * gain + bias
    sigmoid_pre = 1.0 / (1.0 + jnp.exp(-pre))
    return normed, sigmoid_pre * (1.0 + pre * (1.0 - sigmoid_pre))


def sums_kernel(part0, part1, part2, part3, lat0, lat1, lat2, lat3, chan, out):
    cells, channels = lat0.shape
    for q in range(channels // 128):
        lanes = slice(q * 128, q * 128 + 128)
        first = jnp.zeros((8, 128), jnp.float32)
        second = jnp.zeros((8, 128), jnp.float32)
        for part, lat in ((part0, lat0), (part1, lat1), (part2, lat2), (part3, lat3)):
            normed, gate = slope(lat[:, lanes], chan, lanes)
            act = part[q] * gate
            first = first + act.reshape(cells // 8, 8, 128).sum(axis=0)
            second = second + (act * normed).reshape(cells // 8, 8, 128).sum(axis=0)
        out[q : q + 1] = jnp.sum(first, axis=0, keepdims=True)
        out[4 + q : 5 + q] = jnp.sum(second, axis=0, keepdims=True)


def partial_sums(parts, lats, chan):
    return pl.pallas_call(
        sums_kernel,
        out_shape=jax.ShapeDtypeStruct((8, 128), jnp.float32),
        in_specs=[VMEM] * 9,
        out_specs=VMEM,
        compiler_params=pltpu.CompilerParams(vmem_limit_bytes=4 << 20),
        cost_estimate=pl.CostEstimate(
            flops=6_000_000, bytes_accessed=2_600_000, transcendentals=330_000
        ),
    )(*parts, *lats, chan)


def final_kernel(count, sum0, sum1, sum2, sum3, part0, part1, part2, part3, lat, chan, grad, sums):
    cells, channels = lat.shape
    per_group = channels // GROUPS
    total = (sum0[...] + sum1[...] + (sum2[...] + sum3[...])) / count
    sums[...] = total
    row = lax.broadcasted_iota(jnp.int32, (128, 128), 0) // per_group
    col = lax.broadcasted_iota(jnp.int32, (128, 128), 1) // per_group
    same = jnp.where(row == col, 1.0, 0.0)
    gains = jnp.concatenate([chan[2:3, q * 128 : q * 128 + 128] for q in range(4)] * 2, axis=0)
    means = lax.dot_general(
        total * gains,
        same,
        (((1,), (0,)), ((), ())),
        precision=lax.Precision.HIGHEST,
        preferred_element_type=jnp.float32,
    ) / per_group
    for q in range(channels // 128):
        lanes = slice(q * 128, q * 128 + 128)
        normed, gate = slope(lat[:, lanes], chan, lanes)
        up_grad = part0[q] + part1[q] + (part2[q] + part3[q])
        grad[:, lanes] = chan[1:2, lanes] * (
            up_grad * gate * chan[2:3, lanes]
            - means[q : q + 1]
            - normed * means[4 + q : 5 + q]
        )


def final(count, sums, parts, lat, chan):
    return pl.pallas_call(
        functools.partial(final_kernel, count),
        out_shape=[
            jax.ShapeDtypeStruct(lat.shape, jnp.float32),
            jax.ShapeDtypeStruct((8, 128), jnp.float32),
        ],
        in_specs=[VMEM] * 10,
        out_specs=[VMEM] * 2,
        compiler_params=pltpu.CompilerParams(vmem_limit_bytes=4 << 20),
        cost_estimate=pl.CostEstimate(
            flops=2_000_000, bytes_accessed=1_900_000, transcendentals=82_000
        ),
    )(*sums, *parts, lat, chan)


def on_device(latent, norm_gain, norm_bias, conv_weight, cotangent):
    cells, channels = latent.shape[2], latent.shape[3]
    per_group = channels // GROUPS
    cell_count = FRAMES * ROWS * cells
    own = latent[0, 0]

    block = lax.all_to_all(
        message(own, conv_weight.reshape(PLANES, 8, 128)), "z", 0, 0, tiled=True
    )

    msgs = [
        msg if step == 0 else send(msg, "x", step) for step, msg in enumerate(split(cotangent))
    ]
    block, msgs = lax.optimization_barrier((block, msgs))
    pieces = [block] + [send(block, "y", step) for step in range(1, YS)]
    first, last = rims(msgs)
    low = lax.ppermute(last, ROW_AXES, [(i, i + 1) for i in range(ROWS - 1)])
    high = lax.ppermute(first, ROW_AXES, [(i + 1, i) for i in range(ROWS - 1)])
    late, _ = lax.optimization_barrier((own, first))
    lats = [own] + [send(late, "x", step) for step in range(1, FRAMES)]
    lefts = pool(msgs, low, high)
    others = [send(piece, "c", 1) for piece in pieces]
    partial = None
    for steps in ((0, 3), (2, 1)):
        chosen = [piece for step in steps for piece in (pieces[step], others[step])]
        partial = product(chosen, steps, lefts, partial)

    gathered = sum(
        jnp.sum(piece[:, PLANES:].astype(jnp.float32), axis=(0, 1)) for piece in pieces + others
    )
    total = gathered + sum(send(gathered, "x", step) for step in range(1, FRAMES))
    group = total.reshape(2, GROUPS, per_group).sum(axis=2) / (cell_count * per_group)
    group_mean = group[0]
    group_var = group[1] - group_mean * group_mean
    inv_std = lax.rsqrt(group_var + 1e-06)
    chan = jnp.stack(
        [jnp.repeat(group_mean, per_group), jnp.repeat(inv_std, per_group), norm_gain, norm_bias]
    )

    sums = partial_sums(partial, lats, chan)
    parts = [partial[0]] + [send(partial[FRAMES - step], "x", step) for step in range(1, FRAMES)]
    sums = lax.all_to_all(
        jnp.broadcast_to(sums[None], (ROWS, 8, 128)), ROW_AXES, 0, 0, tiled=True
    ).sum(axis=0)
    sums = [sums] + [send(sums, "x", step) for step in range(1, FRAMES)]
    latent_grad, chan_grad = final(cell_count, sums, parts, own, chan)
    bias_grad, gain_grad = chan_grad.reshape(2, channels)
    return (latent_grad.reshape(1, 1, cells, channels), gain_grad, bias_grad)


def solution(mesh):
    fine = Mesh(mesh.devices.reshape(XS, YS, ZS, CS), ("x", "y", "z", "c"))
    image = P("x", ROW_AXES, None, None)
    return jax.shard_map(
        on_device,
        mesh=fine,
        in_specs=(image, P(), P(), P(None, None, None, ROW_AXES, "x"), image),
        out_specs=(image, P(), P()),
        check_vma=False,
    )
```

```python
import functools

import jax
import jax.numpy as jnp
from jax import lax
from jax.experimental import pallas as pl
from jax.experimental.pallas import tpu as pltpu
from jax.sharding import Mesh
from jax.sharding import PartitionSpec as P

GROUPS = 32
XS, YS, ZS, CS = 4, 4, 8, 2
ROWS = YS * ZS * CS
FRAMES = XS
SIZES = {"x": XS, "y": YS, "z": ZS, "c": CS}
ROW_AXES = ("y", "z", "c")
TAPS = 9
PLANES = 3 * TAPS
UNITS = ((0, 1, 2, 3), (0, 1, 2), (0, 1))
VMEM = pl.BlockSpec(memory_space=pltpu.VMEM)
HBM = pl.BlockSpec(memory_space=pltpu.HBM)


def send(value, axis, step):
    size = SIZES[axis]
    return lax.ppermute(value, axis, [(i, (i + step) % size) for i in range(size)])


def pool_kernel(msg0, msg1, msg2, msg3, low, high, out2, out1, out0, sums, pooled):
    cells = out2.shape[1] // FRAMES
    fine = 2 * cells
    place = lax.axis_index("x")
    zero = jnp.zeros((8, 128), jnp.float32)
    for band in range(3):
        sums[band, 0:8] = zero
        sums[band, 8 + fine : 16 + fine] = zero
    for k, msg in enumerate((msg0, msg1, msg2, msg3)):
        frame = lax.rem(place + FRAMES - k, FRAMES)
        upper = msg[0:fine].astype(jnp.float32)
        lower = msg[fine : 2 * fine].astype(jnp.float32)
        sums[0, 8 : 8 + fine] = lower + high[k].astype(jnp.float32)
        sums[1, 8 : 8 + fine] = upper + lower
        sums[2, 8 : 8 + fine] = low[k].astype(jnp.float32) + upper
        for band in range(3):
            at = sums.at[band]
            before = at[pl.ds(7, cells, stride=2), :]
            even = at[pl.ds(8, cells, stride=2), :]
            odd = at[pl.ds(9, cells, stride=2), :]
            after = at[pl.ds(10, cells, stride=2), :]
            pooled[frame, band * 3 + 0] = odd + after
            pooled[frame, band * 3 + 1] = even + odd
            pooled[frame, band * 3 + 2] = before + even
    for tap in range(TAPS):
        lanes = slice(tap * 128, tap * 128 + 128)

        def put(out, unit, value):
            head = value.astype(jnp.bfloat16)
            tail = (value - head.astype(jnp.float32)).astype(jnp.bfloat16)
            out[0, unit * cells : (unit + 1) * cells, lanes] = head
            out[1, unit * cells : (unit + 1) * cells, lanes] = tail

        p0, p1, p2, p3 = (pooled[t, tap] for t in range(FRAMES))
        put(out2, 0, p0)
        put(out2, 1, p1)
        put(out2, 2, p2)
        put(out2, 3, p3)
        p01 = p0 + p1
        put(out1, 0, p01)
        put(out1, 1, p2)
        put(out1, 2, p3)
        put(out0, 0, p01 + p2)
        put(out0, 1, p3)


def pool(msgs, low, high):
    cells = low.shape[1] // 2
    shapes = [
        jax.ShapeDtypeStruct((2, len(units) * cells, TAPS * 128), jnp.bfloat16) for units in UNITS
    ]
    return pl.pallas_call(
        pool_kernel,
        out_shape=shapes,
        in_specs=[VMEM] * 6,
        out_specs=[VMEM] * 3,
        scratch_shapes=[
            pltpu.VMEM((3, 2 * cells + 16, 128), jnp.float32),
            pltpu.VMEM((FRAMES, TAPS, cells, 128), jnp.float32),
        ],
        compiler_params=pltpu.CompilerParams(vmem_limit_bytes=12 << 20),
        cost_estimate=pl.CostEstimate(flops=1_000, bytes_accessed=1_000, transcendentals=0),
    )(*msgs, low, high)


def split_kernel(cot, lat, out0, out1, out2, out3, sems):
    place = lax.axis_index("x")
    fine, cells = cot.shape[2], lat.shape[2]
    copies = []
    for k, out in enumerate((out0, out1, out2, out3)):
        first = pl.multiple_of(lax.rem(place + k, FRAMES) * 128, 128)
        moves = [
            (cot.at[0, row, :, pl.ds(first, 128)], out.at[row * fine : (row + 1) * fine])
            for row in range(2)
        ]
        for q in range(lat.shape[3] // 128):
            start = 2 * fine + q * cells
            moves.append((lat.at[0, 0, :, q * 128 : q * 128 + 128], out.at[start : start + cells]))
        for source, target in moves:
            copies.append(pltpu.make_async_copy(source, target, sems.at[len(copies)]))
    for copy in copies:
        copy.start()
    for copy in copies:
        copy.wait()


def split(cotangent, latent):
    rows = 2 * cotangent.shape[2] + 4 * latent.shape[2]
    return pl.pallas_call(
        split_kernel,
        out_shape=[jax.ShapeDtypeStruct((rows, 128), cotangent.dtype)] * FRAMES,
        in_specs=[HBM] * 2,
        out_specs=[VMEM] * FRAMES,
        scratch_shapes=[pltpu.SemaphoreType.DMA((6 * FRAMES,))],
        compiler_params=pltpu.CompilerParams(vmem_limit_bytes=2 << 20),
        cost_estimate=pl.CostEstimate(flops=0, bytes_accessed=2_600_000, transcendentals=0),
    )(cotangent, latent)


def message_kernel(lat, weight, out, stats, latent, held, sems):
    channels = latent.shape[1]
    copies = [
        pltpu.make_async_copy(lat.at[0, 0], latent, sems.at[0]),
        pltpu.make_async_copy(weight, held, sems.at[1]),
    ]
    for copy in copies:
        copy.start()
    for copy in copies:
        copy.wait()
    for q in range(channels // 128):
        values = latent[:, q * 128 : q * 128 + 128].astype(jnp.float32)
        stats[q : q + 1] = jnp.sum(values, axis=0, keepdims=True)
        stats[4 + q : 5 + q] = jnp.sum(values * values, axis=0, keepdims=True)
    total = stats[...]
    head = total.astype(jnp.bfloat16)
    rest = total - head.astype(jnp.float32)
    middle = rest.astype(jnp.bfloat16)
    last = (rest - middle.astype(jnp.float32)).astype(jnp.bfloat16)
    for z in range(ZS):
        out[z, 0:PLANES] = held[...]
        out[z, PLANES] = head
        out[z, PLANES + 1] = middle
        out[z, PLANES + 2] = last


def message(latent, weight):
    return pl.pallas_call(
        message_kernel,
        out_shape=jax.ShapeDtypeStruct((ZS, PLANES + 3, 8, 128), jnp.bfloat16),
        in_specs=[HBM] * 2,
        out_specs=VMEM,
        scratch_shapes=[
            pltpu.VMEM((8, 128), jnp.float32),
            pltpu.VMEM(latent.shape[2:], latent.dtype),
            pltpu.VMEM(weight.shape, weight.dtype),
            pltpu.SemaphoreType.DMA((2,)),
        ],
        compiler_params=pltpu.CompilerParams(vmem_limit_bytes=3 << 20),
        cost_estimate=pl.CostEstimate(flops=250_000, bytes_accessed=720_000, transcendentals=0),
    )(latent, weight)


def rims_kernel(msg0, msg1, msg2, msg3, first, last):
    for k, msg in enumerate((msg0, msg1, msg2, msg3)):
        fine = first.shape[1]
        first[k] = msg[0:fine]
        last[k] = msg[fine : 2 * fine]


def rims(msgs, fine):
    shape = jax.ShapeDtypeStruct((FRAMES, fine, 128), jnp.bfloat16)
    return pl.pallas_call(
        rims_kernel,
        out_shape=[shape] * 2,
        in_specs=[VMEM] * FRAMES,
        out_specs=[VMEM] * 2,
        compiler_params=pltpu.CompilerParams(vmem_limit_bytes=3 << 20),
        cost_estimate=pl.CostEstimate(flops=0, bytes_accessed=1_000, transcendentals=0),
    )(*msgs)


def product_kernel(steps, aliased, *refs):
    count = CS * len(steps)
    pieces = refs[:count]
    left2, left1, left0 = refs[count : count + 3]
    skip = count + 3 + (FRAMES if aliased else 0)
    outs = refs[skip : skip + FRAMES]
    weights, acc, sems = refs[skip + FRAMES :]
    y, c = lax.axis_index("y"), lax.axis_index("c")
    cells = outs[0].shape[1]
    copies = []
    for index, step in enumerate(steps):
        for side in range(CS):
            core = c if side == 0 else 1 - c
            piece = pieces[index * CS + side]
            for z in range(ZS):
                row = pl.multiple_of(index * 128 + z * (CS * 8) + core * 8, 8)
                copies.append(
                    pltpu.make_async_copy(
                        piece.at[z, 0:PLANES],
                        weights.at[:, pl.ds(row, 8), :],
                        sems.at[len(copies)],
                    )
                )
    for copy in copies:
        copy.start()
    for copy in copies:
        copy.wait()
    for tap, left in ((2, left2), (1, left1), (0, left0)):
        right = jnp.concatenate([weights[tap * TAPS + t] for t in range(TAPS)], axis=1)
        total = None
        for half in range(2):
            part = lax.dot_general(
                left[half], right, (((1,), (1,)), ((), ())), preferred_element_type=jnp.float32
            )
            total = part if total is None else total + part
        if tap == 2:
            acc[...] = total
        else:
            acc[0 : total.shape[0]] += total
    place = lax.axis_index("x")
    for index, step in enumerate(steps):
        source_y = lax.rem(y + YS - step, YS)
        lanes = slice(index * 128, index * 128 + 128)
        for k, out in enumerate(outs):
            frame = lax.rem(place + FRAMES - k, FRAMES)
            out[source_y] = acc[pl.ds(pl.multiple_of(frame * cells, 8), cells), lanes]


def product(pieces, steps, lefts, before):
    cells = lefts[0].shape[1] // FRAMES
    aliased = before is not None
    inputs = [*pieces, *lefts, *(before if aliased else [])]
    return pl.pallas_call(
        functools.partial(product_kernel, steps, aliased),
        out_shape=[jax.ShapeDtypeStruct((YS, cells, 128), jnp.float32)] * FRAMES,
        in_specs=[pl.BlockSpec(memory_space=pl.ANY)] * len(pieces)
        + [VMEM] * (len(inputs) - len(pieces)),
        out_specs=[VMEM] * FRAMES,
        scratch_shapes=[
            pltpu.VMEM((PLANES, len(steps) * 128, 128), jnp.bfloat16),
            pltpu.VMEM((FRAMES * cells, len(steps) * 128), jnp.float32),
            pltpu.SemaphoreType.DMA((CS * ZS * len(steps),)),
        ],
        input_output_aliases={len(pieces) + 3 + k: k for k in range(FRAMES)} if aliased else {},
        compiler_params=pltpu.CompilerParams(vmem_limit_bytes=12 << 20),
        cost_estimate=pl.CostEstimate(
            flops=1_700_000_000, bytes_accessed=9_000_000, transcendentals=0
        ),
    )(*inputs)


def slope(features, chan, lanes):
    mean, inv, gain, bias = (chan[r : r + 1, lanes] for r in range(4))
    normed = (features.astype(jnp.float32) - mean) * inv
    pre = normed * gain + bias
    sigmoid_pre = 1.0 / (1.0 + jnp.exp(-pre))
    return normed, sigmoid_pre * (1.0 + pre * (1.0 - sigmoid_pre))


def sums_kernel(part0, part1, part2, part3, msg0, msg1, msg2, msg3, chan, out, kept):
    cells = part0.shape[1]
    offset = msg0.shape[0] - 4 * cells
    for q in range(4):
        lanes = slice(q * 128, q * 128 + 128)
        first = jnp.zeros((8, 128), jnp.float32)
        second = jnp.zeros((8, 128), jnp.float32)
        for part, msg in ((part0, msg0), (part1, msg1), (part2, msg2), (part3, msg3)):
            start = offset + q * cells
            normed, gate = slope(msg[start : start + cells], chan, lanes)
            act = part[q] * gate
            first = first + act.reshape(cells // 8, 8, 128).sum(axis=0)
            second = second + (act * normed).reshape(cells // 8, 8, 128).sum(axis=0)
        kept[q : q + 1] = jnp.sum(first, axis=0, keepdims=True)
        kept[4 + q : 5 + q] = jnp.sum(second, axis=0, keepdims=True)
    total = kept[...]
    for i in range(out.shape[0]):
        out[i] = total


def partial_sums(parts, msgs, chan):
    return pl.pallas_call(
        sums_kernel,
        out_shape=jax.ShapeDtypeStruct((ROWS, 8, 128), jnp.float32),
        in_specs=[VMEM] * 9,
        out_specs=VMEM,
        scratch_shapes=[pltpu.VMEM((8, 128), jnp.float32)],
        compiler_params=pltpu.CompilerParams(vmem_limit_bytes=4 << 20),
        cost_estimate=pl.CostEstimate(
            flops=6_000_000, bytes_accessed=2_900_000, transcendentals=330_000
        ),
    )(*parts, *msgs, chan)


def final_kernel(count, sum0, sum1, sum2, sum3, part0, part1, part2, part3, lat, chan, grad, gain_grad, bias_grad):
    cells, channels = lat.shape
    per_group = channels // GROUPS
    total = (sum0[...] + sum1[...] + (sum2[...] + sum3[...])) / count
    for q in range(4):
        bias_grad[q * 128 : q * 128 + 128] = total[q]
        gain_grad[q * 128 : q * 128 + 128] = total[4 + q]
    row = lax.broadcasted_iota(jnp.int32, (128, 128), 0) // per_group
    col = lax.broadcasted_iota(jnp.int32, (128, 128), 1) // per_group
    same = jnp.where(row == col, 1.0, 0.0)
    gains = jnp.concatenate([chan[2:3, q * 128 : q * 128 + 128] for q in range(4)] * 2, axis=0)
    means = lax.dot_general(
        total * gains,
        same,
        (((1,), (0,)), ((), ())),
        precision=lax.Precision.HIGHEST,
        preferred_element_type=jnp.float32,
    ) / per_group
    for q in range(channels // 128):
        lanes = slice(q * 128, q * 128 + 128)
        normed, gate = slope(lat[:, lanes], chan, lanes)
        up_grad = part0[q] + part1[q] + (part2[q] + part3[q])
        grad[:, lanes] = chan[1:2, lanes] * (
            up_grad * gate * chan[2:3, lanes]
            - means[q : q + 1]
            - normed * means[4 + q : 5 + q]
        )


def final(count, sums, parts, lat, chan):
    return pl.pallas_call(
        functools.partial(final_kernel, count),
        out_shape=[
            jax.ShapeDtypeStruct(lat.shape, jnp.float32),
            jax.ShapeDtypeStruct((lat.shape[1],), jnp.float32),
            jax.ShapeDtypeStruct((lat.shape[1],), jnp.float32),
        ],
        in_specs=[VMEM] * 10,
        out_specs=[VMEM] * 3,
        compiler_params=pltpu.CompilerParams(vmem_limit_bytes=4 << 20),
        cost_estimate=pl.CostEstimate(
            flops=2_000_000, bytes_accessed=1_900_000, transcendentals=82_000
        ),
    )(*sums, *parts, lat, chan)


def on_device(latent, norm_gain, norm_bias, conv_weight, cotangent):
    cells, channels = latent.shape[2], latent.shape[3]
    per_group = channels // GROUPS
    cell_count = FRAMES * ROWS * cells
    own = latent[0, 0]

    block = lax.all_to_all(
        message(latent, conv_weight.reshape(PLANES, 8, 128)), "z", 0, 0, tiled=True
    )
    pieces = [block] + [send(block, "y", step) for step in range(1, YS)]

    msgs = [
        msg if step == 0 else send(msg, "x", step)
        for step, msg in enumerate(split(cotangent, latent))
    ]
    first, last = rims(msgs, cotangent.shape[2])
    low = lax.ppermute(last, ROW_AXES, [(i, i + 1) for i in range(ROWS - 1)])
    high = lax.ppermute(first, ROW_AXES, [(i + 1, i) for i in range(ROWS - 1)])
    lefts = pool(msgs, low, high)
    others = [send(piece, "c", 1) for piece in pieces]
    partial = None
    for steps in ((0, 3), (2, 1)):
        chosen = [piece for step in steps for piece in (pieces[step], others[step])]
        partial = product(chosen, steps, lefts, partial)

    gathered = sum(
        jnp.sum(piece[:, PLANES:].astype(jnp.float32), axis=(0, 1)) for piece in pieces + others
    )
    total = gathered + sum(send(gathered, "x", step) for step in range(1, FRAMES))
    group = total.reshape(2, GROUPS, per_group).sum(axis=2) / (cell_count * per_group)
    group_mean = group[0]
    group_var = group[1] - group_mean * group_mean
    inv_std = lax.rsqrt(group_var + 1e-06)
    chan = jnp.stack(
        [jnp.repeat(group_mean, per_group), jnp.repeat(inv_std, per_group), norm_gain, norm_bias]
    )

    sums = partial_sums(partial, msgs, chan)
    parts = [partial[0]] + [send(partial[FRAMES - step], "x", step) for step in range(1, FRAMES)]
    sums = lax.all_to_all(sums, ROW_AXES, 0, 0, tiled=True).sum(axis=0)
    sums = [sums] + [send(sums, "x", step) for step in range(1, FRAMES)]
    latent_grad, gain_grad, bias_grad = final(cell_count, sums, parts, own, chan)
    return (latent_grad.reshape(1, 1, cells, channels), gain_grad, bias_grad)


def solution(mesh):
    fine = Mesh(mesh.devices.reshape(XS, YS, ZS, CS), ("x", "y", "z", "c"))
    image = P("x", ROW_AXES, None, None)
    return jax.shard_map(
        on_device,
        mesh=fine,
        in_specs=(image, P(), P(), P(None, None, None, ROW_AXES, "x"), image),
        out_specs=(image, P(), P()),
        check_vma=False,
    )
```

```python
import functools

import jax
import jax.numpy as jnp
from jax import lax
from jax.experimental import pallas as pl
from jax.experimental.pallas import tpu as pltpu
from jax.sharding import Mesh
from jax.sharding import PartitionSpec as P

GROUPS = 32
XS, YS, ZS, CS = 4, 4, 8, 2
ROWS = YS * ZS * CS
FRAMES = XS
SIZES = {"x": XS, "y": YS, "z": ZS, "c": CS}
ROW_AXES = ("y", "z", "c")
TAPS = 9
PLANES = 3 * TAPS
UNITS = ((0, 1, 2, 3), (0, 1, 2), (0, 1))
VMEM = pl.BlockSpec(memory_space=pltpu.VMEM)
HBM = pl.BlockSpec(memory_space=pltpu.HBM)


def send(value, axis, step):
    size = SIZES[axis]
    return lax.ppermute(value, axis, [(i, (i + step) % size) for i in range(size)])


def pool_kernel(msg0, msg1, msg2, msg3, low, high, out2, out1, out0, sums, pooled):
    cells = out2.shape[1] // FRAMES
    fine = 2 * cells
    place = lax.axis_index("x")
    zero = jnp.zeros((8, 128), jnp.float32)
    for band in range(3):
        sums[band, 0:8] = zero
        sums[band, 8 + fine : 16 + fine] = zero
    for k, msg in enumerate((msg0, msg1, msg2, msg3)):
        frame = lax.rem(place + FRAMES - k, FRAMES)
        upper = msg[0:fine].astype(jnp.float32)
        lower = msg[fine : 2 * fine].astype(jnp.float32)
        sums[0, 8 : 8 + fine] = lower + high[k].astype(jnp.float32)
        sums[1, 8 : 8 + fine] = upper + lower
        sums[2, 8 : 8 + fine] = low[k].astype(jnp.float32) + upper
        for band in range(3):
            at = sums.at[band]
            before = at[pl.ds(7, cells, stride=2), :]
            even = at[pl.ds(8, cells, stride=2), :]
            odd = at[pl.ds(9, cells, stride=2), :]
            after = at[pl.ds(10, cells, stride=2), :]
            pooled[frame, band * 3 + 0] = odd + after
            pooled[frame, band * 3 + 1] = even + odd
            pooled[frame, band * 3 + 2] = before + even
    for tap in range(TAPS):
        lanes = slice(tap * 128, tap * 128 + 128)

        def put(out, unit, value):
            head = value.astype(jnp.bfloat16)
            tail = (value - head.astype(jnp.float32)).astype(jnp.bfloat16)
            out[0, unit * cells : (unit + 1) * cells, lanes] = head
            out[1, unit * cells : (unit + 1) * cells, lanes] = tail

        p0, p1, p2, p3 = (pooled[t, tap] for t in range(FRAMES))
        put(out2, 0, p0)
        put(out2, 1, p1)
        put(out2, 2, p2)
        put(out2, 3, p3)
        p01 = p0 + p1
        put(out1, 0, p01)
        put(out1, 1, p2)
        put(out1, 2, p3)
        put(out0, 0, p01 + p2)
        put(out0, 1, p3)


def pool(msgs, low, high):
    cells = low.shape[1] // 2
    shapes = [
        jax.ShapeDtypeStruct((2, len(units) * cells, TAPS * 128), jnp.bfloat16) for units in UNITS
    ]
    return pl.pallas_call(
        pool_kernel,
        out_shape=shapes,
        in_specs=[VMEM] * 6,
        out_specs=[VMEM] * 3,
        scratch_shapes=[
            pltpu.VMEM((3, 2 * cells + 16, 128), jnp.float32),
            pltpu.VMEM((FRAMES, TAPS, cells, 128), jnp.float32),
        ],
        compiler_params=pltpu.CompilerParams(vmem_limit_bytes=12 << 20),
        cost_estimate=pl.CostEstimate(flops=1_000, bytes_accessed=1_000, transcendentals=0),
    )(*msgs, low, high)


def split_kernel(cot, out0, out1, out2, out3, sems):
    place = lax.axis_index("x")
    fine = cot.shape[2]
    copies = []
    for k, out in enumerate((out0, out1, out2, out3)):
        first = pl.multiple_of(lax.rem(place + k, FRAMES) * 128, 128)
        moves = [
            (cot.at[0, row, :, pl.ds(first, 128)], out.at[row * fine : (row + 1) * fine])
            for row in range(2)
        ]
        for source, target in moves:
            copies.append(pltpu.make_async_copy(source, target, sems.at[len(copies)]))
    for copy in copies:
        copy.start()
    for copy in copies:
        copy.wait()


def split(cotangent):
    rows = 2 * cotangent.shape[2]
    return pl.pallas_call(
        split_kernel,
        out_shape=[jax.ShapeDtypeStruct((rows, 128), cotangent.dtype)] * FRAMES,
        in_specs=[HBM],
        out_specs=[VMEM] * FRAMES,
        scratch_shapes=[pltpu.SemaphoreType.DMA((2 * FRAMES,))],
        compiler_params=pltpu.CompilerParams(vmem_limit_bytes=2 << 20),
        cost_estimate=pl.CostEstimate(flops=0, bytes_accessed=1_300_000, transcendentals=0),
    )(cotangent)


def message_kernel(lat, weight, out, stats, latent, held, sems):
    channels = latent.shape[1]
    copies = [
        pltpu.make_async_copy(lat.at[0, 0], latent, sems.at[0]),
        pltpu.make_async_copy(weight, held, sems.at[1]),
    ]
    for copy in copies:
        copy.start()
    for copy in copies:
        copy.wait()
    for q in range(channels // 128):
        values = latent[:, q * 128 : q * 128 + 128].astype(jnp.float32)
        stats[q : q + 1] = jnp.sum(values, axis=0, keepdims=True)
        stats[4 + q : 5 + q] = jnp.sum(values * values, axis=0, keepdims=True)
    total = stats[...]
    head = total.astype(jnp.bfloat16)
    rest = total - head.astype(jnp.float32)
    middle = rest.astype(jnp.bfloat16)
    last = (rest - middle.astype(jnp.float32)).astype(jnp.bfloat16)
    for z in range(ZS):
        out[z, 0:PLANES] = held[...]
        out[z, PLANES] = head
        out[z, PLANES + 1] = middle
        out[z, PLANES + 2] = last


def message(latent, weight):
    return pl.pallas_call(
        message_kernel,
        out_shape=jax.ShapeDtypeStruct((ZS, PLANES + 3, 8, 128), jnp.bfloat16),
        in_specs=[HBM] * 2,
        out_specs=VMEM,
        scratch_shapes=[
            pltpu.VMEM((8, 128), jnp.float32),
            pltpu.VMEM(latent.shape[2:], latent.dtype),
            pltpu.VMEM(weight.shape, weight.dtype),
            pltpu.SemaphoreType.DMA((2,)),
        ],
        compiler_params=pltpu.CompilerParams(vmem_limit_bytes=3 << 20),
        cost_estimate=pl.CostEstimate(flops=250_000, bytes_accessed=720_000, transcendentals=0),
    )(latent, weight)


def share_kernel(total, lat, out):
    cells = lat.shape[0]
    for q in range(4):
        out[q * cells : (q + 1) * cells] = lat[:, q * 128 : q * 128 + 128]
    rest = jnp.concatenate([total[...], jnp.zeros((8, 128), jnp.float32)], axis=0)
    for p in range(3):
        part = rest.astype(jnp.bfloat16)
        out[4 * cells + 16 * p : 4 * cells + 16 * p + 16] = part
        rest = rest - part.astype(jnp.float32)


def share(total, lat):
    return pl.pallas_call(
        share_kernel,
        out_shape=jax.ShapeDtypeStruct((4 * lat.shape[0] + 48, 128), jnp.bfloat16),
        in_specs=[VMEM] * 2,
        out_specs=VMEM,
        compiler_params=pltpu.CompilerParams(vmem_limit_bytes=2 << 20),
        cost_estimate=pl.CostEstimate(flops=10_000, bytes_accessed=340_000, transcendentals=0),
    )(total, lat)


def rims_kernel(msg0, msg1, msg2, msg3, first, last):
    for k, msg in enumerate((msg0, msg1, msg2, msg3)):
        fine = first.shape[1]
        first[k] = msg[0:fine]
        last[k] = msg[fine : 2 * fine]


def rims(msgs, fine):
    shape = jax.ShapeDtypeStruct((FRAMES, fine, 128), jnp.bfloat16)
    return pl.pallas_call(
        rims_kernel,
        out_shape=[shape] * 2,
        in_specs=[VMEM] * FRAMES,
        out_specs=[VMEM] * 2,
        compiler_params=pltpu.CompilerParams(vmem_limit_bytes=3 << 20),
        cost_estimate=pl.CostEstimate(flops=0, bytes_accessed=1_000, transcendentals=0),
    )(*msgs)


def product_kernel(steps, aliased, *refs):
    count = CS * len(steps)
    pieces = refs[:count]
    left2, left1, left0 = refs[count : count + 3]
    skip = count + 3 + (FRAMES if aliased else 0)
    outs = refs[skip : skip + FRAMES]
    weights, acc, sems = refs[skip + FRAMES :]
    y, c = lax.axis_index("y"), lax.axis_index("c")
    cells = outs[0].shape[1]
    copies = []
    for index, step in enumerate(steps):
        for side in range(CS):
            core = c if side == 0 else 1 - c
            piece = pieces[index * CS + side]
            for z in range(ZS):
                source_z = z + core * (ZS - 1 - 2 * z)
                row = pl.multiple_of(index * 128 + source_z * (CS * 8) + core * 8, 8)
                copies.append(
                    pltpu.make_async_copy(
                        piece.at[z, 0:PLANES],
                        weights.at[:, pl.ds(row, 8), :],
                        sems.at[len(copies)],
                    )
                )
    for copy in copies:
        copy.start()
    for copy in copies:
        copy.wait()
    for tap, left in ((2, left2), (1, left1), (0, left0)):
        right = jnp.concatenate([weights[tap * TAPS + t] for t in range(TAPS)], axis=1)
        total = None
        for half in range(2):
            part = lax.dot_general(
                left[half], right, (((1,), (1,)), ((), ())), preferred_element_type=jnp.float32
            )
            total = part if total is None else total + part
        if tap == 2:
            acc[...] = total
        else:
            acc[0 : total.shape[0]] += total
    place = lax.axis_index("x")
    for index, step in enumerate(steps):
        source_y = lax.rem(y + YS - step, YS)
        lanes = slice(index * 128, index * 128 + 128)
        for k, out in enumerate(outs):
            frame = lax.rem(place + FRAMES - k, FRAMES)
            out[source_y] = acc[pl.ds(pl.multiple_of(frame * cells, 8), cells), lanes]


def product(pieces, steps, lefts, before):
    cells = lefts[0].shape[1] // FRAMES
    aliased = before is not None
    inputs = [*pieces, *lefts, *(before if aliased else [])]
    return pl.pallas_call(
        functools.partial(product_kernel, steps, aliased),
        out_shape=[jax.ShapeDtypeStruct((YS, cells, 128), jnp.float32)] * FRAMES,
        in_specs=[pl.BlockSpec(memory_space=pl.ANY)] * len(pieces)
        + [VMEM] * (len(inputs) - len(pieces)),
        out_specs=[VMEM] * FRAMES,
        scratch_shapes=[
            pltpu.VMEM((PLANES, len(steps) * 128, 128), jnp.bfloat16),
            pltpu.VMEM((FRAMES * cells, len(steps) * 128), jnp.float32),
            pltpu.SemaphoreType.DMA((CS * ZS * len(steps),)),
        ],
        input_output_aliases={len(pieces) + 3 + k: k for k in range(FRAMES)} if aliased else {},
        compiler_params=pltpu.CompilerParams(vmem_limit_bytes=12 << 20),
        cost_estimate=pl.CostEstimate(
            flops=1_700_000_000, bytes_accessed=9_000_000, transcendentals=0
        ),
    )(*inputs)


def slope(features, chan, lanes):
    mean, inv, gain, bias = (chan[r : r + 1, lanes] for r in range(4))
    normed = (features.astype(jnp.float32) - mean) * inv
    pre = normed * gain + bias
    sigmoid_pre = 1.0 / (1.0 + jnp.exp(-pre))
    return normed, sigmoid_pre * (1.0 + pre * (1.0 - sigmoid_pre))


def sums_kernel(part0, part1, part2, part3, msg0, msg1, msg2, msg3, chan, out, kept):
    cells = part0.shape[1]
    for q in range(4):
        lanes = slice(q * 128, q * 128 + 128)
        first = jnp.zeros((8, 128), jnp.float32)
        second = jnp.zeros((8, 128), jnp.float32)
        for part, msg in ((part0, msg0), (part1, msg1), (part2, msg2), (part3, msg3)):
            start = q * cells
            normed, gate = slope(msg[start : start + cells], chan, lanes)
            act = part[q] * gate
            first = first + act.reshape(cells // 8, 8, 128).sum(axis=0)
            second = second + (act * normed).reshape(cells // 8, 8, 128).sum(axis=0)
        kept[q : q + 1] = jnp.sum(first, axis=0, keepdims=True)
        kept[4 + q : 5 + q] = jnp.sum(second, axis=0, keepdims=True)
    total = kept[...]
    for i in range(out.shape[0]):
        out[i] = total


def partial_sums(parts, msgs, chan):
    return pl.pallas_call(
        sums_kernel,
        out_shape=jax.ShapeDtypeStruct((ROWS, 8, 128), jnp.float32),
        in_specs=[VMEM] * 9,
        out_specs=VMEM,
        scratch_shapes=[pltpu.VMEM((8, 128), jnp.float32)],
        compiler_params=pltpu.CompilerParams(vmem_limit_bytes=4 << 20),
        cost_estimate=pl.CostEstimate(
            flops=6_000_000, bytes_accessed=2_900_000, transcendentals=330_000
        ),
    )(*parts, *msgs, chan)


def final_kernel(count, sum0, sum1, sum2, sum3, part0, part1, part2, part3, lat, chan, grad, gain_grad, bias_grad):
    cells, channels = lat.shape
    per_group = channels // GROUPS
    total = (sum0[...] + sum1[...] + (sum2[...] + sum3[...])) / count
    for q in range(4):
        bias_grad[q * 128 : q * 128 + 128] = total[q]
        gain_grad[q * 128 : q * 128 + 128] = total[4 + q]
    row = lax.broadcasted_iota(jnp.int32, (128, 128), 0) // per_group
    col = lax.broadcasted_iota(jnp.int32, (128, 128), 1) // per_group
    same = jnp.where(row == col, 1.0, 0.0)
    gains = jnp.concatenate([chan[2:3, q * 128 : q * 128 + 128] for q in range(4)] * 2, axis=0)
    means = lax.dot_general(
        total * gains,
        same,
        (((1,), (0,)), ((), ())),
        precision=lax.Precision.HIGHEST,
        preferred_element_type=jnp.float32,
    ) / per_group
    for q in range(channels // 128):
        lanes = slice(q * 128, q * 128 + 128)
        normed, gate = slope(lat[:, lanes], chan, lanes)
        up_grad = part0[q] + part1[q] + (part2[q] + part3[q])
        grad[:, lanes] = chan[1:2, lanes] * (
            up_grad * gate * chan[2:3, lanes]
            - means[q : q + 1]
            - normed * means[4 + q : 5 + q]
        )


def final(count, sums, parts, lat, chan):
    return pl.pallas_call(
        functools.partial(final_kernel, count),
        out_shape=[
            jax.ShapeDtypeStruct(lat.shape, jnp.float32),
            jax.ShapeDtypeStruct((lat.shape[1],), jnp.float32),
            jax.ShapeDtypeStruct((lat.shape[1],), jnp.float32),
        ],
        in_specs=[VMEM] * 10,
        out_specs=[VMEM] * 3,
        compiler_params=pltpu.CompilerParams(vmem_limit_bytes=4 << 20),
        cost_estimate=pl.CostEstimate(
            flops=2_000_000, bytes_accessed=1_900_000, transcendentals=82_000
        ),
    )(*sums, *parts, lat, chan)


def on_device(latent, norm_gain, norm_bias, conv_weight, cotangent):
    cells, channels = latent.shape[2], latent.shape[3]
    per_group = channels // GROUPS
    cell_count = FRAMES * ROWS * cells
    own = latent[0, 0]

    block = lax.all_to_all(
        message(latent, conv_weight.reshape(PLANES, 8, 128)),
        ("z", "c"),
        0,
        0,
        axis_index_groups=[
            [z * CS for z in range(ZS)],
            [z * CS + 1 for z in reversed(range(ZS))],
        ],
        tiled=True,
    )

    msgs = [
        msg if step == 0 else send(msg, "x", step)
        for step, msg in enumerate(split(cotangent))
    ]
    block, msgs = lax.optimization_barrier((block, msgs))
    pieces = [block] + [send(block, "y", step) for step in range(1, YS)]
    first_rows, last_rows = rims(msgs, cotangent.shape[2])
    low = lax.ppermute(last_rows, ROW_AXES, [(i, i + 1) for i in range(ROWS - 1)])
    high = lax.ppermute(first_rows, ROW_AXES, [(i + 1, i) for i in range(ROWS - 1)])
    lefts = pool(msgs, low, high)
    others = [send(piece, "c", 1) for piece in pieces]
    partial = None
    for steps in ((0, 3), (2, 1)):
        chosen = [piece for step in steps for piece in (pieces[step], others[step])]
        partial = product(chosen, steps, lefts, partial)

    gathered = sum(
        jnp.sum(piece[:, PLANES:].astype(jnp.float32), axis=(0, 1)) for piece in pieces + others
    )
    shared = share(gathered, own)
    lats = [shared] + [send(shared, "x", step) for step in range(1, FRAMES)]
    total = sum(
        lat[first : first + 8].astype(jnp.float32)
        for lat in lats
        for first in range(4 * cells, 4 * cells + 48, 16)
    )
    group = total.reshape(2, GROUPS, per_group).sum(axis=2) / (cell_count * per_group)
    group_mean = group[0]
    group_var = group[1] - group_mean * group_mean
    inv_std = lax.rsqrt(group_var + 1e-06)
    chan = jnp.stack(
        [jnp.repeat(group_mean, per_group), jnp.repeat(inv_std, per_group), norm_gain, norm_bias]
    )

    sums = partial_sums(partial, lats, chan)
    parts = [partial[0]] + [send(partial[FRAMES - step], "x", step) for step in range(1, FRAMES)]
    sums = lax.all_to_all(sums, ROW_AXES, 0, 0, tiled=True).sum(axis=0)
    sums = [sums] + [send(sums, "x", step) for step in range(1, FRAMES)]
    latent_grad, gain_grad, bias_grad = final(cell_count, sums, parts, own, chan)
    return (latent_grad.reshape(1, 1, cells, channels), gain_grad, bias_grad)


def solution(mesh):
    fine = Mesh(mesh.devices.reshape(XS, YS, ZS, CS), ("x", "y", "z", "c"))
    image = P("x", ROW_AXES, None, None)
    return jax.shard_map(
        on_device,
        mesh=fine,
        in_specs=(image, P(), P(), P(None, None, None, ROW_AXES, "x"), image),
        out_specs=(image, P(), P()),
        check_vma=False,
    )
```

```python
import functools

import jax
import jax.numpy as jnp
from jax import lax
from jax.experimental import pallas as pl
from jax.experimental.pallas import tpu as pltpu
from jax.sharding import Mesh
from jax.sharding import PartitionSpec as P

GROUPS = 32
XS, YS, ZS, CS = 4, 4, 8, 2
ROWS = YS * ZS * CS
FRAMES = XS
SIZES = {"x": XS, "y": YS, "z": ZS, "c": CS}
ROW_AXES = ("y", "z", "c")
TAPS = 9
PLANES = 3 * TAPS
UNITS = ((0, 1, 2, 3), (0, 1, 2), (0, 1))
VMEM = pl.BlockSpec(memory_space=pltpu.VMEM)
HBM = pl.BlockSpec(memory_space=pltpu.HBM)


def send(value, axis, step):
    size = SIZES[axis]
    return lax.ppermute(value, axis, [(i, (i + step) % size) for i in range(size)])


def pool_kernel(msg0, msg1, msg2, msg3, cross, inner, out2, out1, out0, sums, pooled):
    cells = out2.shape[1] // FRAMES
    fine = 2 * cells
    place, c = lax.axis_index("x"), lax.axis_index("c")
    mine = pl.ds(pl.multiple_of(c * fine, fine), fine)
    other = pl.ds(pl.multiple_of((1 - c) * fine, fine), fine)
    zero = jnp.zeros((8, 128), jnp.float32)
    for band in range(3):
        sums[band, 0:8] = zero
        sums[band, 8 + fine : 16 + fine] = zero
    for k, msg in enumerate((msg0, msg1, msg2, msg3)):
        frame = lax.rem(place + FRAMES - k, FRAMES)
        upper = msg[0:fine].astype(jnp.float32)
        lower = msg[fine : 2 * fine].astype(jnp.float32)
        sums[1, 8 : 8 + fine] = upper + lower
        sums[2 - 2 * c, 8 : 8 + fine] = (
            msg[mine].astype(jnp.float32) + cross[k].astype(jnp.float32)
        )
        sums[2 * c, 8 : 8 + fine] = msg[other].astype(jnp.float32) + inner[k].astype(jnp.float32)
        for band in range(3):
            at = sums.at[band]
            before = at[pl.ds(7, cells, stride=2), :]
            even = at[pl.ds(8, cells, stride=2), :]
            odd = at[pl.ds(9, cells, stride=2), :]
            after = at[pl.ds(10, cells, stride=2), :]
            pooled[frame, band * 3 + 0] = odd + after
            pooled[frame, band * 3 + 1] = even + odd
            pooled[frame, band * 3 + 2] = before + even
    for tap in range(TAPS):
        lanes = slice(tap * 128, tap * 128 + 128)

        def put(out, unit, value):
            head = value.astype(jnp.bfloat16)
            tail = (value - head.astype(jnp.float32)).astype(jnp.bfloat16)
            out[0, unit * cells : (unit + 1) * cells, lanes] = head
            out[1, unit * cells : (unit + 1) * cells, lanes] = tail

        p0, p1, p2, p3 = (pooled[t, tap] for t in range(FRAMES))
        put(out2, 0, p0)
        put(out2, 1, p1)
        put(out2, 2, p2)
        put(out2, 3, p3)
        p01 = p0 + p1
        put(out1, 0, p01)
        put(out1, 1, p2)
        put(out1, 2, p3)
        put(out0, 0, p01 + p2)
        put(out0, 1, p3)


def pool(msgs, cross, inner):
    cells = cross.shape[1] // 2
    shapes = [
        jax.ShapeDtypeStruct((2, len(units) * cells, TAPS * 128), jnp.bfloat16) for units in UNITS
    ]
    return pl.pallas_call(
        pool_kernel,
        out_shape=shapes,
        in_specs=[VMEM] * 6,
        out_specs=[VMEM] * 3,
        scratch_shapes=[
            pltpu.VMEM((3, 2 * cells + 16, 128), jnp.float32),
            pltpu.VMEM((FRAMES, TAPS, cells, 128), jnp.float32),
        ],
        compiler_params=pltpu.CompilerParams(vmem_limit_bytes=12 << 20),
        cost_estimate=pl.CostEstimate(flops=1_000, bytes_accessed=1_000, transcendentals=0),
    )(*msgs, cross, inner)


def split_kernel(cot, out0, out1, out2, out3, sems):
    place = lax.axis_index("x")
    fine = cot.shape[2]
    copies = []
    for k, out in enumerate((out0, out1, out2, out3)):
        first = pl.multiple_of(lax.rem(place + k, FRAMES) * 128, 128)
        moves = [
            (cot.at[0, row, :, pl.ds(first, 128)], out.at[row * fine : (row + 1) * fine])
            for row in range(2)
        ]
        for source, target in moves:
            copies.append(pltpu.make_async_copy(source, target, sems.at[len(copies)]))
    for copy in copies:
        copy.start()
    for copy in copies:
        copy.wait()


def split(cotangent):
    rows = 2 * cotangent.shape[2]
    return pl.pallas_call(
        split_kernel,
        out_shape=[jax.ShapeDtypeStruct((rows, 128), cotangent.dtype)] * FRAMES,
        in_specs=[HBM],
        out_specs=[VMEM] * FRAMES,
        scratch_shapes=[pltpu.SemaphoreType.DMA((2 * FRAMES,))],
        compiler_params=pltpu.CompilerParams(vmem_limit_bytes=2 << 20),
        cost_estimate=pl.CostEstimate(flops=0, bytes_accessed=1_300_000, transcendentals=0),
    )(cotangent)


def message_kernel(lat, weight, out, stats, latent, held, sems):
    channels = latent.shape[1]
    copies = [
        pltpu.make_async_copy(lat.at[0, 0], latent, sems.at[0]),
        pltpu.make_async_copy(weight, held, sems.at[1]),
    ]
    for copy in copies:
        copy.start()
    for copy in copies:
        copy.wait()
    for q in range(channels // 128):
        values = latent[:, q * 128 : q * 128 + 128].astype(jnp.float32)
        stats[q : q + 1] = jnp.sum(values, axis=0, keepdims=True)
        stats[4 + q : 5 + q] = jnp.sum(values * values, axis=0, keepdims=True)
    total = stats[...]
    head = total.astype(jnp.bfloat16)
    rest = total - head.astype(jnp.float32)
    middle = rest.astype(jnp.bfloat16)
    last = (rest - middle.astype(jnp.float32)).astype(jnp.bfloat16)
    for z in range(ZS):
        out[z, 0:PLANES] = held[...]
        out[z, PLANES] = head
        out[z, PLANES + 1] = middle
        out[z, PLANES + 2] = last


def message(latent, weight):
    return pl.pallas_call(
        message_kernel,
        out_shape=jax.ShapeDtypeStruct((ZS, PLANES + 3, 8, 128), jnp.bfloat16),
        in_specs=[HBM] * 2,
        out_specs=VMEM,
        scratch_shapes=[
            pltpu.VMEM((8, 128), jnp.float32),
            pltpu.VMEM(latent.shape[2:], latent.dtype),
            pltpu.VMEM(weight.shape, weight.dtype),
            pltpu.SemaphoreType.DMA((2,)),
        ],
        compiler_params=pltpu.CompilerParams(vmem_limit_bytes=3 << 20),
        cost_estimate=pl.CostEstimate(flops=250_000, bytes_accessed=720_000, transcendentals=0),
    )(latent, weight)


def share_kernel(total, lat, out):
    cells = lat.shape[0]
    for q in range(4):
        out[q * cells : (q + 1) * cells] = lat[:, q * 128 : q * 128 + 128]
    rest = jnp.concatenate([total[...], jnp.zeros((8, 128), jnp.float32)], axis=0)
    for p in range(3):
        part = rest.astype(jnp.bfloat16)
        out[4 * cells + 16 * p : 4 * cells + 16 * p + 16] = part
        rest = rest - part.astype(jnp.float32)


def share(total, lat):
    return pl.pallas_call(
        share_kernel,
        out_shape=jax.ShapeDtypeStruct((4 * lat.shape[0] + 48, 128), jnp.bfloat16),
        in_specs=[VMEM] * 2,
        out_specs=VMEM,
        compiler_params=pltpu.CompilerParams(vmem_limit_bytes=2 << 20),
        cost_estimate=pl.CostEstimate(flops=10_000, bytes_accessed=340_000, transcendentals=0),
    )(total, lat)


def rims_kernel(msg0, msg1, msg2, msg3, cross, inner):
    fine = cross.shape[1]
    c = lax.axis_index("c")
    for k, msg in enumerate((msg0, msg1, msg2, msg3)):
        cross[k] = msg[pl.ds(pl.multiple_of(c * fine, fine), fine)]
        inner[k] = msg[pl.ds(pl.multiple_of((1 - c) * fine, fine), fine)]


def rims(msgs, fine):
    shape = jax.ShapeDtypeStruct((FRAMES, fine, 128), jnp.bfloat16)
    return pl.pallas_call(
        rims_kernel,
        out_shape=[shape] * 2,
        in_specs=[VMEM] * FRAMES,
        out_specs=[VMEM] * 2,
        compiler_params=pltpu.CompilerParams(vmem_limit_bytes=3 << 20),
        cost_estimate=pl.CostEstimate(flops=0, bytes_accessed=1_000, transcendentals=0),
    )(*msgs)


def product_kernel(steps, aliased, *refs):
    count = CS * len(steps)
    pieces = refs[:count]
    left2, left1, left0 = refs[count : count + 3]
    skip = count + 3 + (FRAMES if aliased else 0)
    outs = refs[skip : skip + FRAMES]
    weights, acc, sems = refs[skip + FRAMES :]
    y, c = lax.axis_index("y"), lax.axis_index("c")
    cells = outs[0].shape[1]
    copies = []
    for index, step in enumerate(steps):
        for side in range(CS):
            core = c if side == 0 else 1 - c
            piece = pieces[index * CS + side]
            for z in range(ZS):
                source_z = z + core * (ZS - 1 - 2 * z)
                row = pl.multiple_of(index * 128 + source_z * (CS * 8) + core * 8, 8)
                copies.append(
                    pltpu.make_async_copy(
                        piece.at[z, 0:PLANES],
                        weights.at[:, pl.ds(row, 8), :],
                        sems.at[len(copies)],
                    )
                )
    for copy in copies:
        copy.start()
    for copy in copies:
        copy.wait()
    for tap, left in ((2, left2), (1, left1), (0, left0)):
        right = jnp.concatenate([weights[tap * TAPS + t] for t in range(TAPS)], axis=1)
        total = None
        for half in range(2):
            part = lax.dot_general(
                left[half], right, (((1,), (1,)), ((), ())), preferred_element_type=jnp.float32
            )
            total = part if total is None else total + part
        if tap == 2:
            acc[...] = total
        else:
            acc[0 : total.shape[0]] += total
    place = lax.axis_index("x")
    for index, step in enumerate(steps):
        source_y = lax.rem(y + YS - step, YS)
        lanes = slice(index * 128, index * 128 + 128)
        for k, out in enumerate(outs):
            frame = lax.rem(place + FRAMES - k, FRAMES)
            out[source_y] = acc[pl.ds(pl.multiple_of(frame * cells, 8), cells), lanes]


def product(pieces, steps, lefts, before):
    cells = lefts[0].shape[1] // FRAMES
    aliased = before is not None
    inputs = [*pieces, *lefts, *(before if aliased else [])]
    return pl.pallas_call(
        functools.partial(product_kernel, steps, aliased),
        out_shape=[jax.ShapeDtypeStruct((YS, cells, 128), jnp.float32)] * FRAMES,
        in_specs=[pl.BlockSpec(memory_space=pl.ANY)] * len(pieces)
        + [VMEM] * (len(inputs) - len(pieces)),
        out_specs=[VMEM] * FRAMES,
        scratch_shapes=[
            pltpu.VMEM((PLANES, len(steps) * 128, 128), jnp.bfloat16),
            pltpu.VMEM((FRAMES * cells, len(steps) * 128), jnp.float32),
            pltpu.SemaphoreType.DMA((CS * ZS * len(steps),)),
        ],
        input_output_aliases={len(pieces) + 3 + k: k for k in range(FRAMES)} if aliased else {},
        compiler_params=pltpu.CompilerParams(vmem_limit_bytes=12 << 20),
        cost_estimate=pl.CostEstimate(
            flops=1_700_000_000, bytes_accessed=9_000_000, transcendentals=0
        ),
    )(*inputs)


def slope(features, chan, lanes):
    mean, inv, gain, bias = (chan[r : r + 1, lanes] for r in range(4))
    normed = (features.astype(jnp.float32) - mean) * inv
    pre = normed * gain + bias
    sigmoid_pre = 1.0 / (1.0 + jnp.exp(-pre))
    return normed, sigmoid_pre * (1.0 + pre * (1.0 - sigmoid_pre))


def sums_kernel(part0, part1, part2, part3, msg0, msg1, msg2, msg3, chan, kept):
    cells = part0.shape[1]
    for q in range(4):
        lanes = slice(q * 128, q * 128 + 128)
        first = jnp.zeros((8, 128), jnp.float32)
        second = jnp.zeros((8, 128), jnp.float32)
        for part, msg in ((part0, msg0), (part1, msg1), (part2, msg2), (part3, msg3)):
            start = q * cells
            normed, gate = slope(msg[start : start + cells], chan, lanes)
            act = part[q] * gate
            first = first + act.reshape(cells // 8, 8, 128).sum(axis=0)
            second = second + (act * normed).reshape(cells // 8, 8, 128).sum(axis=0)
        kept[q : q + 1] = jnp.sum(first, axis=0, keepdims=True)
        kept[4 + q : 5 + q] = jnp.sum(second, axis=0, keepdims=True)


def partial_sums(parts, msgs, chan):
    return pl.pallas_call(
        sums_kernel,
        out_shape=jax.ShapeDtypeStruct((8, 128), jnp.float32),
        in_specs=[VMEM] * 9,
        out_specs=VMEM,
        compiler_params=pltpu.CompilerParams(vmem_limit_bytes=4 << 20),
        cost_estimate=pl.CostEstimate(
            flops=6_000_000, bytes_accessed=2_900_000, transcendentals=330_000
        ),
    )(*parts, *msgs, chan)


def final_kernel(count, sum0, sum1, sum2, sum3, part0, part1, part2, part3, lat, chan, grad, gain_grad, bias_grad):
    cells, channels = lat.shape
    per_group = channels // GROUPS
    total = (sum0[...] + sum1[...] + (sum2[...] + sum3[...])) / count
    for q in range(4):
        bias_grad[q * 128 : q * 128 + 128] = total[q]
        gain_grad[q * 128 : q * 128 + 128] = total[4 + q]
    row = lax.broadcasted_iota(jnp.int32, (128, 128), 0) // per_group
    col = lax.broadcasted_iota(jnp.int32, (128, 128), 1) // per_group
    same = jnp.where(row == col, 1.0, 0.0)
    gains = jnp.concatenate([chan[2:3, q * 128 : q * 128 + 128] for q in range(4)] * 2, axis=0)
    means = lax.dot_general(
        total * gains,
        same,
        (((1,), (0,)), ((), ())),
        precision=lax.Precision.HIGHEST,
        preferred_element_type=jnp.float32,
    ) / per_group
    for q in range(channels // 128):
        lanes = slice(q * 128, q * 128 + 128)
        normed, gate = slope(lat[:, lanes], chan, lanes)
        up_grad = part0[q] + part1[q] + (part2[q] + part3[q])
        grad[:, lanes] = chan[1:2, lanes] * (
            up_grad * gate * chan[2:3, lanes]
            - means[q : q + 1]
            - normed * means[4 + q : 5 + q]
        )


def final(count, sums, parts, lat, chan):
    return pl.pallas_call(
        functools.partial(final_kernel, count),
        out_shape=[
            jax.ShapeDtypeStruct(lat.shape, jnp.float32),
            jax.ShapeDtypeStruct((lat.shape[1],), jnp.float32),
            jax.ShapeDtypeStruct((lat.shape[1],), jnp.float32),
        ],
        in_specs=[VMEM] * 10,
        out_specs=[VMEM] * 3,
        compiler_params=pltpu.CompilerParams(vmem_limit_bytes=4 << 20),
        cost_estimate=pl.CostEstimate(
            flops=2_000_000, bytes_accessed=1_900_000, transcendentals=82_000
        ),
    )(*sums, *parts, lat, chan)


def on_device(latent, norm_gain, norm_bias, conv_weight, cotangent):
    cells, channels = latent.shape[2], latent.shape[3]
    per_group = channels // GROUPS
    cell_count = FRAMES * ROWS * cells
    own = latent[0, 0]

    block = lax.all_to_all(
        message(latent, conv_weight.reshape(PLANES, 8, 128)),
        ("z", "c"),
        0,
        0,
        axis_index_groups=[
            [z * CS for z in range(ZS)],
            [z * CS + 1 for z in reversed(range(ZS))],
        ],
        tiled=True,
    )

    msgs = [
        msg if step == 0 else send(msg, "x", step)
        for step, msg in enumerate(split(cotangent))
    ]
    block, msgs = lax.optimization_barrier((block, msgs))
    pieces = [block] + [send(block, "y", step) for step in range(1, YS)]
    first_rows, last_rows = rims(msgs, cotangent.shape[2])
    pairs = [(i, i + 1) for i in range(1, ROWS - 1, CS)]
    cross = lax.ppermute(first_rows, ROW_AXES, pairs + [(j, i) for i, j in pairs])
    inner = send(last_rows, "c", 1)
    lefts = pool(msgs, cross, inner)
    others = [send(piece, "c", 1) for piece in pieces]
    partial = None
    for steps in ((0, 3), (2, 1)):
        chosen = [piece for step in steps for piece in (pieces[step], others[step])]
        partial = product(chosen, steps, lefts, partial)

    gathered = sum(
        jnp.sum(piece[:, PLANES:].astype(jnp.float32), axis=(0, 1)) for piece in pieces + others
    )
    shared = share(gathered, own)
    lats = [shared] + [send(shared, "x", step) for step in range(1, FRAMES)]
    total = sum(
        lat[first : first + 8].astype(jnp.float32)
        for lat in lats
        for first in range(4 * cells, 4 * cells + 48, 16)
    )
    group = total.reshape(2, GROUPS, per_group).sum(axis=2) / (cell_count * per_group)
    group_mean = group[0]
    group_var = group[1] - group_mean * group_mean
    inv_std = lax.rsqrt(group_var + 1e-06)
    chan = jnp.stack(
        [jnp.repeat(group_mean, per_group), jnp.repeat(inv_std, per_group), norm_gain, norm_bias]
    )

    sums = partial_sums(partial, lats, chan)
    parts = [partial[0]] + [send(partial[FRAMES - step], "x", step) for step in range(1, FRAMES)]
    sums = sums + send(sums, "c", 1)
    sums = jnp.broadcast_to(sums[None], (YS * ZS, 8, 128))
    sums = lax.all_to_all(
        sums,
        ROW_AXES,
        0,
        0,
        axis_index_groups=[list(range(0, ROWS, CS)), list(range(ROWS - 1, 0, -CS))],
        tiled=True,
    ).sum(axis=0)
    sums = [sums] + [send(sums, "x", step) for step in range(1, FRAMES)]
    latent_grad, gain_grad, bias_grad = final(cell_count, sums, parts, own, chan)
    return (latent_grad.reshape(1, 1, cells, channels), gain_grad, bias_grad)


def solution(mesh):
    fine = Mesh(mesh.devices.reshape(XS, YS, ZS, CS), ("x", "y", "z", "c"))
    image = P("x", ROW_AXES, None, None)
    return jax.shard_map(
        on_device,
        mesh=fine,
        in_specs=(image, P(), P(), P(None, None, None, ROW_AXES, "x"), image),
        out_specs=(image, P(), P()),
        check_vma=False,
    )
```

```python
import functools

import jax
import jax.numpy as jnp
from jax import lax
from jax.experimental import pallas as pl
from jax.experimental.pallas import tpu as pltpu
from jax.sharding import Mesh
from jax.sharding import PartitionSpec as P

GROUPS = 32
XS, YS, ZS, CS = 4, 4, 8, 2
ROWS = YS * ZS * CS
FRAMES = XS
SIZES = {"x": XS, "y": YS, "z": ZS, "c": CS}
ROW_AXES = ("y", "z", "c")
TAPS = 9
PLANES = 3 * TAPS
UNITS = ((0, 1, 2, 3), (0, 1, 2), (0, 1))
VMEM = pl.BlockSpec(memory_space=pltpu.VMEM)
HBM = pl.BlockSpec(memory_space=pltpu.HBM)


def send(value, axis, step):
    size = SIZES[axis]
    return lax.ppermute(value, axis, [(i, (i + step) % size) for i in range(size)])


def pool_kernel(msg0, msg1, msg2, msg3, cross, inner, out2, out1, out0, sums, pooled):
    cells = out2.shape[1] // FRAMES
    fine = 2 * cells
    place, c = lax.axis_index("x"), lax.axis_index("c")
    mine = pl.ds(pl.multiple_of(c * fine, fine), fine)
    other = pl.ds(pl.multiple_of((1 - c) * fine, fine), fine)
    zero = jnp.zeros((8, 128), jnp.float32)
    for band in range(3):
        sums[band, 0:8] = zero
        sums[band, 8 + fine : 16 + fine] = zero
    for k, msg in enumerate((msg0, msg1, msg2, msg3)):
        frame = lax.rem(place + FRAMES - k, FRAMES)
        upper = msg[0:fine].astype(jnp.float32)
        lower = msg[fine : 2 * fine].astype(jnp.float32)
        sums[1, 8 : 8 + fine] = upper + lower
        sums[2 - 2 * c, 8 : 8 + fine] = (
            msg[mine].astype(jnp.float32) + cross[k].astype(jnp.float32)
        )
        sums[2 * c, 8 : 8 + fine] = msg[other].astype(jnp.float32) + inner[k].astype(jnp.float32)
        for band in range(3):
            at = sums.at[band]
            before = at[pl.ds(7, cells, stride=2), :]
            even = at[pl.ds(8, cells, stride=2), :]
            odd = at[pl.ds(9, cells, stride=2), :]
            after = at[pl.ds(10, cells, stride=2), :]
            pooled[frame, band * 3 + 0] = odd + after
            pooled[frame, band * 3 + 1] = even + odd
            pooled[frame, band * 3 + 2] = before + even
    for tap in range(TAPS):
        lanes = slice(tap * 128, tap * 128 + 128)

        def put(out, unit, value):
            head = value.astype(jnp.bfloat16)
            tail = (value - head.astype(jnp.float32)).astype(jnp.bfloat16)
            out[0, unit * cells : (unit + 1) * cells, lanes] = head
            out[1, unit * cells : (unit + 1) * cells, lanes] = tail

        p0, p1, p2, p3 = (pooled[t, tap] for t in range(FRAMES))
        put(out2, 0, p0)
        put(out2, 1, p1)
        put(out2, 2, p2)
        put(out2, 3, p3)
        p01 = p0 + p1
        put(out1, 0, p01)
        put(out1, 1, p2)
        put(out1, 2, p3)
        put(out0, 0, p01 + p2)
        put(out0, 1, p3)


def pool(msgs, cross, inner):
    cells = cross.shape[1] // 2
    shapes = [
        jax.ShapeDtypeStruct((2, len(units) * cells, TAPS * 128), jnp.bfloat16) for units in UNITS
    ]
    return pl.pallas_call(
        pool_kernel,
        out_shape=shapes,
        in_specs=[VMEM] * 6,
        out_specs=[VMEM] * 3,
        scratch_shapes=[
            pltpu.VMEM((3, 2 * cells + 16, 128), jnp.float32),
            pltpu.VMEM((FRAMES, TAPS, cells, 128), jnp.float32),
        ],
        compiler_params=pltpu.CompilerParams(vmem_limit_bytes=12 << 20),
        cost_estimate=pl.CostEstimate(flops=1_000, bytes_accessed=1_000, transcendentals=0),
    )(*msgs, cross, inner)


def split_kernel(cot, out0, out1, out2, out3, sems):
    place = lax.axis_index("x")
    fine = cot.shape[2]
    copies = []
    for k, out in enumerate((out0, out1, out2, out3)):
        first = pl.multiple_of(lax.rem(place + k, FRAMES) * 128, 128)
        moves = [
            (cot.at[0, row, :, pl.ds(first, 128)], out.at[row * fine : (row + 1) * fine])
            for row in range(2)
        ]
        for source, target in moves:
            copies.append(pltpu.make_async_copy(source, target, sems.at[len(copies)]))
    for copy in copies:
        copy.start()
    for copy in copies:
        copy.wait()


def split(cotangent):
    rows = 2 * cotangent.shape[2]
    return pl.pallas_call(
        split_kernel,
        out_shape=[jax.ShapeDtypeStruct((rows, 128), cotangent.dtype)] * FRAMES,
        in_specs=[HBM],
        out_specs=[VMEM] * FRAMES,
        scratch_shapes=[pltpu.SemaphoreType.DMA((2 * FRAMES,))],
        compiler_params=pltpu.CompilerParams(vmem_limit_bytes=2 << 20),
        cost_estimate=pl.CostEstimate(flops=0, bytes_accessed=1_300_000, transcendentals=0),
    )(cotangent)


def message_kernel(lat, weight, out, stats, latent, held, sems):
    channels = latent.shape[1]
    copies = [
        pltpu.make_async_copy(lat.at[0, 0], latent, sems.at[0]),
        pltpu.make_async_copy(weight, held, sems.at[1]),
    ]
    for copy in copies:
        copy.start()
    for copy in copies:
        copy.wait()
    for q in range(channels // 128):
        values = latent[:, q * 128 : q * 128 + 128].astype(jnp.float32)
        stats[q : q + 1] = jnp.sum(values, axis=0, keepdims=True)
        stats[4 + q : 5 + q] = jnp.sum(values * values, axis=0, keepdims=True)
    total = stats[...]
    head = total.astype(jnp.bfloat16)
    rest = total - head.astype(jnp.float32)
    middle = rest.astype(jnp.bfloat16)
    last = (rest - middle.astype(jnp.float32)).astype(jnp.bfloat16)
    for z in range(ZS):
        out[z, 0:PLANES] = held[...]
        out[z, PLANES] = head
        out[z, PLANES + 1] = middle
        out[z, PLANES + 2] = last


def message(latent, weight):
    return pl.pallas_call(
        message_kernel,
        out_shape=jax.ShapeDtypeStruct((ZS, PLANES + 3, 8, 128), jnp.bfloat16),
        in_specs=[HBM] * 2,
        out_specs=VMEM,
        scratch_shapes=[
            pltpu.VMEM((8, 128), jnp.float32),
            pltpu.VMEM(latent.shape[2:], latent.dtype),
            pltpu.VMEM(weight.shape, weight.dtype),
            pltpu.SemaphoreType.DMA((2,)),
        ],
        compiler_params=pltpu.CompilerParams(vmem_limit_bytes=59 << 20),
        cost_estimate=pl.CostEstimate(flops=250_000, bytes_accessed=720_000, transcendentals=0),
    )(latent, weight)


def share_kernel(total, lat, out):
    cells = lat.shape[0]
    for q in range(4):
        out[q * cells : (q + 1) * cells] = lat[:, q * 128 : q * 128 + 128]
    rest = jnp.concatenate([total[...], jnp.zeros((8, 128), jnp.float32)], axis=0)
    for p in range(3):
        part = rest.astype(jnp.bfloat16)
        out[4 * cells + 16 * p : 4 * cells + 16 * p + 16] = part
        rest = rest - part.astype(jnp.float32)


def share(total, lat):
    return pl.pallas_call(
        share_kernel,
        out_shape=jax.ShapeDtypeStruct((4 * lat.shape[0] + 48, 128), jnp.bfloat16),
        in_specs=[VMEM] * 2,
        out_specs=VMEM,
        compiler_params=pltpu.CompilerParams(vmem_limit_bytes=2 << 20),
        cost_estimate=pl.CostEstimate(flops=10_000, bytes_accessed=340_000, transcendentals=0),
    )(total, lat)


def rims_kernel(msg0, msg1, msg2, msg3, cross, inner):
    fine = cross.shape[1]
    c = lax.axis_index("c")
    for k, msg in enumerate((msg0, msg1, msg2, msg3)):
        cross[k] = msg[pl.ds(pl.multiple_of(c * fine, fine), fine)]
        inner[k] = msg[pl.ds(pl.multiple_of((1 - c) * fine, fine), fine)]


def rims(msgs, fine):
    shape = jax.ShapeDtypeStruct((FRAMES, fine, 128), jnp.bfloat16)
    return pl.pallas_call(
        rims_kernel,
        out_shape=[shape] * 2,
        in_specs=[VMEM] * FRAMES,
        out_specs=[VMEM] * 2,
        compiler_params=pltpu.CompilerParams(vmem_limit_bytes=3 << 20),
        cost_estimate=pl.CostEstimate(flops=0, bytes_accessed=1_000, transcendentals=0),
    )(*msgs)


def product_kernel(steps, aliased, *refs):
    count = CS * len(steps)
    pieces = refs[:count]
    left2, left1, left0 = refs[count : count + 3]
    skip = count + 3 + (FRAMES if aliased else 0)
    outs = refs[skip : skip + FRAMES]
    weights, acc, sems = refs[skip + FRAMES :]
    y, c = lax.axis_index("y"), lax.axis_index("c")
    cells = outs[0].shape[1]
    copies = []
    for index, step in enumerate(steps):
        for side in range(CS):
            core = c if side == 0 else 1 - c
            piece = pieces[index * CS + side]
            for z in range(ZS):
                source_z = z + core * (ZS - 1 - 2 * z)
                row = pl.multiple_of(index * 128 + source_z * (CS * 8) + core * 8, 8)
                copies.append(
                    pltpu.make_async_copy(
                        piece.at[z, 0:PLANES],
                        weights.at[:, pl.ds(row, 8), :],
                        sems.at[len(copies)],
                    )
                )
    for copy in copies:
        copy.start()
    for copy in copies:
        copy.wait()
    for tap, left in ((2, left2), (1, left1), (0, left0)):
        right = jnp.concatenate([weights[tap * TAPS + t] for t in range(TAPS)], axis=1)
        total = None
        for half in range(2):
            part = lax.dot_general(
                left[half], right, (((1,), (1,)), ((), ())), preferred_element_type=jnp.float32
            )
            total = part if total is None else total + part
        if tap == 2:
            acc[...] = total
        else:
            acc[0 : total.shape[0]] += total
    place = lax.axis_index("x")
    for index, step in enumerate(steps):
        source_y = lax.rem(y + YS - step, YS)
        lanes = slice(index * 128, index * 128 + 128)
        for k, out in enumerate(outs):
            frame = lax.rem(place + FRAMES - k, FRAMES)
            out[source_y] = acc[pl.ds(pl.multiple_of(frame * cells, 8), cells), lanes]


def product(pieces, steps, lefts, before):
    cells = lefts[0].shape[1] // FRAMES
    aliased = before is not None
    inputs = [*pieces, *lefts, *(before if aliased else [])]
    return pl.pallas_call(
        functools.partial(product_kernel, steps, aliased),
        out_shape=[jax.ShapeDtypeStruct((YS, cells, 128), jnp.float32)] * FRAMES,
        in_specs=[pl.BlockSpec(memory_space=pl.ANY)] * len(pieces)
        + [VMEM] * (len(inputs) - len(pieces)),
        out_specs=[VMEM] * FRAMES,
        scratch_shapes=[
            pltpu.VMEM((PLANES, len(steps) * 128, 128), jnp.bfloat16),
            pltpu.VMEM((FRAMES * cells, len(steps) * 128), jnp.float32),
            pltpu.SemaphoreType.DMA((CS * ZS * len(steps),)),
        ],
        input_output_aliases={len(pieces) + 3 + k: k for k in range(FRAMES)} if aliased else {},
        compiler_params=pltpu.CompilerParams(vmem_limit_bytes=12 << 20),
        cost_estimate=pl.CostEstimate(
            flops=1_700_000_000, bytes_accessed=9_000_000, transcendentals=0
        ),
    )(*inputs)


def slope(features, chan, lanes):
    mean, inv, gain, bias = (chan[r : r + 1, lanes] for r in range(4))
    normed = (features.astype(jnp.float32) - mean) * inv
    pre = normed * gain + bias
    sigmoid_pre = 1.0 / (1.0 + jnp.exp(-pre))
    return normed, sigmoid_pre * (1.0 + pre * (1.0 - sigmoid_pre))


def sums_kernel(part0, part1, part2, part3, msg0, msg1, msg2, msg3, chan, kept):
    cells = part0.shape[1]
    for q in range(4):
        lanes = slice(q * 128, q * 128 + 128)
        first = jnp.zeros((8, 128), jnp.float32)
        second = jnp.zeros((8, 128), jnp.float32)
        for part, msg in ((part0, msg0), (part1, msg1), (part2, msg2), (part3, msg3)):
            start = q * cells
            normed, gate = slope(msg[start : start + cells], chan, lanes)
            act = part[q] * gate
            first = first + act.reshape(cells // 8, 8, 128).sum(axis=0)
            second = second + (act * normed).reshape(cells // 8, 8, 128).sum(axis=0)
        kept[q : q + 1] = jnp.sum(first, axis=0, keepdims=True)
        kept[4 + q : 5 + q] = jnp.sum(second, axis=0, keepdims=True)


def partial_sums(parts, msgs, chan):
    return pl.pallas_call(
        sums_kernel,
        out_shape=jax.ShapeDtypeStruct((8, 128), jnp.float32),
        in_specs=[VMEM] * 9,
        out_specs=VMEM,
        compiler_params=pltpu.CompilerParams(vmem_limit_bytes=4 << 20),
        cost_estimate=pl.CostEstimate(
            flops=6_000_000, bytes_accessed=2_900_000, transcendentals=330_000
        ),
    )(*parts, *msgs, chan)


def final_kernel(count, sum0, sum1, sum2, sum3, part0, part1, part2, part3, lat, chan, grad, gain_grad, bias_grad):
    cells, channels = lat.shape
    per_group = channels // GROUPS
    total = (sum0[...] + sum1[...] + (sum2[...] + sum3[...])) / count
    for q in range(4):
        bias_grad[q * 128 : q * 128 + 128] = total[q]
        gain_grad[q * 128 : q * 128 + 128] = total[4 + q]
    row = lax.broadcasted_iota(jnp.int32, (128, 128), 0) // per_group
    col = lax.broadcasted_iota(jnp.int32, (128, 128), 1) // per_group
    same = jnp.where(row == col, 1.0, 0.0)
    gains = jnp.concatenate([chan[2:3, q * 128 : q * 128 + 128] for q in range(4)] * 2, axis=0)
    means = lax.dot_general(
        total * gains,
        same,
        (((1,), (0,)), ((), ())),
        precision=lax.Precision.HIGHEST,
        preferred_element_type=jnp.float32,
    ) / per_group
    for q in range(channels // 128):
        lanes = slice(q * 128, q * 128 + 128)
        normed, gate = slope(lat[:, lanes], chan, lanes)
        up_grad = part0[q] + part1[q] + (part2[q] + part3[q])
        grad[:, lanes] = chan[1:2, lanes] * (
            up_grad * gate * chan[2:3, lanes]
            - means[q : q + 1]
            - normed * means[4 + q : 5 + q]
        )


def final(count, sums, parts, lat, chan):
    return pl.pallas_call(
        functools.partial(final_kernel, count),
        out_shape=[
            jax.ShapeDtypeStruct(lat.shape, jnp.float32),
            jax.ShapeDtypeStruct((lat.shape[1],), jnp.float32),
            jax.ShapeDtypeStruct((lat.shape[1],), jnp.float32),
        ],
        in_specs=[VMEM] * 10,
        out_specs=[VMEM] * 3,
        compiler_params=pltpu.CompilerParams(vmem_limit_bytes=4 << 20),
        cost_estimate=pl.CostEstimate(
            flops=2_000_000, bytes_accessed=1_900_000, transcendentals=82_000
        ),
    )(*sums, *parts, lat, chan)


def on_device(latent, norm_gain, norm_bias, conv_weight, cotangent):
    cells, channels = latent.shape[2], latent.shape[3]
    per_group = channels // GROUPS
    cell_count = FRAMES * ROWS * cells
    own = latent[0, 0]

    block = lax.all_to_all(
        message(latent, conv_weight.reshape(PLANES, 8, 128)),
        ("z", "c"),
        0,
        0,
        axis_index_groups=[
            [z * CS for z in range(ZS)],
            [z * CS + 1 for z in reversed(range(ZS))],
        ],
        tiled=True,
    )

    msgs = [
        msg if step == 0 else send(msg, "x", step)
        for step, msg in enumerate(split(cotangent))
    ]
    block, msgs = lax.optimization_barrier((block, msgs))
    pieces = [block] + [send(block, "y", step) for step in range(1, YS)]
    first_rows, last_rows = rims(msgs, cotangent.shape[2])
    pairs = [(i, i + 1) for i in range(1, ROWS - 1, CS)]
    cross = lax.ppermute(first_rows, ROW_AXES, pairs + [(j, i) for i, j in pairs])
    inner = send(last_rows, "c", 1)
    lefts = pool(msgs, cross, inner)
    others = [send(piece, "c", 1) for piece in pieces]
    partial = None
    for steps in ((0, 3), (2, 1)):
        chosen = [piece for step in steps for piece in (pieces[step], others[step])]
        partial = product(chosen, steps, lefts, partial)

    gathered = sum(
        jnp.sum(piece[:, PLANES:].astype(jnp.float32), axis=(0, 1)) for piece in pieces + others
    )
    shared = share(gathered, own)
    lats = [shared] + [send(shared, "x", step) for step in range(1, FRAMES)]
    total = sum(
        lat[first : first + 8].astype(jnp.float32)
        for lat in lats
        for first in range(4 * cells, 4 * cells + 48, 16)
    )
    group = total.reshape(2, GROUPS, per_group).sum(axis=2) / (cell_count * per_group)
    group_mean = group[0]
    group_var = group[1] - group_mean * group_mean
    inv_std = lax.rsqrt(group_var + 1e-06)
    chan = jnp.stack(
        [jnp.repeat(group_mean, per_group), jnp.repeat(inv_std, per_group), norm_gain, norm_bias]
    )

    sums = partial_sums(partial, lats, chan)
    parts = [partial[0]] + [send(partial[FRAMES - step], "x", step) for step in range(1, FRAMES)]
    sums = sums + send(sums, "c", 1)
    sums = jnp.broadcast_to(sums[None], (YS * ZS, 8, 128))
    sums = lax.all_to_all(
        sums,
        ROW_AXES,
        0,
        0,
        axis_index_groups=[list(range(0, ROWS, CS)), list(range(ROWS - 1, 0, -CS))],
        tiled=True,
    ).sum(axis=0)
    sums = [sums] + [send(sums, "x", step) for step in range(1, FRAMES)]
    latent_grad, gain_grad, bias_grad = final(cell_count, sums, parts, own, chan)
    return (latent_grad.reshape(1, 1, cells, channels), gain_grad, bias_grad)


def solution(mesh):
    fine = Mesh(mesh.devices.reshape(XS, YS, ZS, CS), ("x", "y", "z", "c"))
    image = P("x", ROW_AXES, None, None)
    return jax.shard_map(
        on_device,
        mesh=fine,
        in_specs=(image, P(), P(), P(None, None, None, ROW_AXES, "x"), image),
        out_specs=(image, P(), P()),
        check_vma=False,
    )
```

```python
import functools

import jax
import jax.numpy as jnp
from jax import lax
from jax.experimental import pallas as pl
from jax.experimental.pallas import tpu as pltpu
from jax.sharding import Mesh
from jax.sharding import PartitionSpec as P

GROUPS = 32
XS, YS, ZS, CS = 4, 4, 8, 2
ROWS = YS * ZS * CS
FRAMES = XS
SIZES = {"x": XS, "y": YS, "z": ZS, "c": CS}
ROW_AXES = ("y", "z", "c")
TAPS = 9
PLANES = 3 * TAPS
UNITS = ((0, 1, 2, 3), (0, 1, 2), (0, 1))
VMEM = pl.BlockSpec(memory_space=pltpu.VMEM)
HBM = pl.BlockSpec(memory_space=pltpu.HBM)


def send(value, axis, step):
    size = SIZES[axis]
    return lax.ppermute(value, axis, [(i, (i + step) % size) for i in range(size)])


def pool_kernel(msg0, msg1, msg2, msg3, cross, inner, out2, out1, out0, sums, pooled):
    cells = out2.shape[1] // FRAMES
    fine = 2 * cells
    place, c = lax.axis_index("x"), lax.axis_index("c")
    mine = pl.ds(pl.multiple_of(c * fine, fine), fine)
    other = pl.ds(pl.multiple_of((1 - c) * fine, fine), fine)
    zero = jnp.zeros((8, 128), jnp.float32)
    for band in range(3):
        sums[band, 0:8] = zero
        sums[band, 8 + fine : 16 + fine] = zero
    for k, msg in enumerate((msg0, msg1, msg2, msg3)):
        frame = lax.rem(place + FRAMES - k, FRAMES)
        upper = msg[0:fine].astype(jnp.float32)
        lower = msg[fine : 2 * fine].astype(jnp.float32)
        sums[1, 8 : 8 + fine] = upper + lower
        sums[2 - 2 * c, 8 : 8 + fine] = (
            msg[mine].astype(jnp.float32) + cross[k].astype(jnp.float32)
        )
        sums[2 * c, 8 : 8 + fine] = msg[other].astype(jnp.float32) + inner[k].astype(jnp.float32)
        for band in range(3):
            at = sums.at[band]
            before = at[pl.ds(7, cells, stride=2), :]
            even = at[pl.ds(8, cells, stride=2), :]
            odd = at[pl.ds(9, cells, stride=2), :]
            after = at[pl.ds(10, cells, stride=2), :]
            pooled[frame, band * 3 + 0] = odd + after
            pooled[frame, band * 3 + 1] = even + odd
            pooled[frame, band * 3 + 2] = before + even
    for tap in range(TAPS):
        lanes = slice(tap * 128, tap * 128 + 128)

        def put(out, unit, value):
            head = value.astype(jnp.bfloat16)
            tail = (value - head.astype(jnp.float32)).astype(jnp.bfloat16)
            out[0, unit * cells : (unit + 1) * cells, lanes] = head
            out[1, unit * cells : (unit + 1) * cells, lanes] = tail

        p0, p1, p2, p3 = (pooled[t, tap] for t in range(FRAMES))
        put(out2, 0, p0)
        put(out2, 1, p1)
        put(out2, 2, p2)
        put(out2, 3, p3)
        p01 = p0 + p1
        put(out1, 0, p01)
        put(out1, 1, p2)
        put(out1, 2, p3)
        put(out0, 0, p01 + p2)
        put(out0, 1, p3)


def pool(msgs, cross, inner):
    cells = cross.shape[1] // 2
    shapes = [
        jax.ShapeDtypeStruct((2, len(units) * cells, TAPS * 128), jnp.bfloat16) for units in UNITS
    ]
    return pl.pallas_call(
        pool_kernel,
        out_shape=shapes,
        in_specs=[VMEM] * 6,
        out_specs=[VMEM] * 3,
        scratch_shapes=[
            pltpu.VMEM((3, 2 * cells + 16, 128), jnp.float32),
            pltpu.VMEM((FRAMES, TAPS, cells, 128), jnp.float32),
        ],
        compiler_params=pltpu.CompilerParams(vmem_limit_bytes=12 << 20),
        cost_estimate=pl.CostEstimate(flops=1_000, bytes_accessed=1_000, transcendentals=0),
    )(*msgs, cross, inner)


def split_kernel(cot, out0, out1, out2, out3, sems):
    place = lax.axis_index("x")
    fine = cot.shape[2]
    copies = []
    for k, out in enumerate((out0, out1, out2, out3)):
        first = pl.multiple_of(lax.rem(place + k, FRAMES) * 128, 128)
        moves = [
            (cot.at[0, row, :, pl.ds(first, 128)], out.at[row * fine : (row + 1) * fine])
            for row in range(2)
        ]
        for source, target in moves:
            copies.append(pltpu.make_async_copy(source, target, sems.at[len(copies)]))
    for copy in copies:
        copy.start()
    for copy in copies:
        copy.wait()


def split(cotangent):
    rows = 2 * cotangent.shape[2]
    return pl.pallas_call(
        split_kernel,
        out_shape=[jax.ShapeDtypeStruct((rows, 128), cotangent.dtype)] * FRAMES,
        in_specs=[HBM],
        out_specs=[VMEM] * FRAMES,
        scratch_shapes=[pltpu.SemaphoreType.DMA((2 * FRAMES,))],
        compiler_params=pltpu.CompilerParams(vmem_limit_bytes=2 << 20),
        cost_estimate=pl.CostEstimate(flops=0, bytes_accessed=1_300_000, transcendentals=0),
    )(cotangent)


def message_kernel(lat, weight, out, stats, latent, held, sems):
    channels = latent.shape[1]
    copies = [
        pltpu.make_async_copy(lat.at[0, 0], latent, sems.at[0]),
        pltpu.make_async_copy(weight, held, sems.at[1]),
    ]
    for copy in copies:
        copy.start()
    for copy in copies:
        copy.wait()
    for q in range(channels // 128):
        values = latent[:, q * 128 : q * 128 + 128].astype(jnp.float32)
        stats[q : q + 1] = jnp.sum(values, axis=0, keepdims=True)
        stats[4 + q : 5 + q] = jnp.sum(values * values, axis=0, keepdims=True)
    total = stats[...]
    head = total.astype(jnp.bfloat16)
    rest = total - head.astype(jnp.float32)
    middle = rest.astype(jnp.bfloat16)
    last = (rest - middle.astype(jnp.float32)).astype(jnp.bfloat16)
    for z in range(ZS):
        out[z, 0:PLANES] = held[...]
        out[z, PLANES] = head
        out[z, PLANES + 1] = middle
        out[z, PLANES + 2] = last


def message(latent, weight):
    return pl.pallas_call(
        message_kernel,
        out_shape=jax.ShapeDtypeStruct((ZS, PLANES + 3, 8, 128), jnp.bfloat16),
        in_specs=[HBM] * 2,
        out_specs=VMEM,
        scratch_shapes=[
            pltpu.VMEM((8, 128), jnp.float32),
            pltpu.VMEM(latent.shape[2:], latent.dtype),
            pltpu.VMEM(weight.shape, weight.dtype),
            pltpu.SemaphoreType.DMA((2,)),
        ],
        compiler_params=pltpu.CompilerParams(vmem_limit_bytes=59 << 20),
        cost_estimate=pl.CostEstimate(flops=250_000, bytes_accessed=720_000, transcendentals=0),
    )(latent, weight)


def share_kernel(total, lat, out):
    cells = lat.shape[0]
    for q in range(4):
        out[q * cells : (q + 1) * cells] = lat[:, q * 128 : q * 128 + 128]
    rest = jnp.concatenate([total[...], jnp.zeros((8, 128), jnp.float32)], axis=0)
    for p in range(3):
        part = rest.astype(jnp.bfloat16)
        out[4 * cells + 16 * p : 4 * cells + 16 * p + 16] = part
        rest = rest - part.astype(jnp.float32)


def share(total, lat):
    return pl.pallas_call(
        share_kernel,
        out_shape=jax.ShapeDtypeStruct((4 * lat.shape[0] + 48, 128), jnp.bfloat16),
        in_specs=[VMEM] * 2,
        out_specs=VMEM,
        compiler_params=pltpu.CompilerParams(vmem_limit_bytes=2 << 20),
        cost_estimate=pl.CostEstimate(flops=10_000, bytes_accessed=340_000, transcendentals=0),
    )(total, lat)


def rims_kernel(msg0, msg1, msg2, msg3, cross, inner):
    fine = cross.shape[1]
    c = lax.axis_index("c")
    for k, msg in enumerate((msg0, msg1, msg2, msg3)):
        cross[k] = msg[pl.ds(pl.multiple_of(c * fine, fine), fine)]
        inner[k] = msg[pl.ds(pl.multiple_of((1 - c) * fine, fine), fine)]


def rims(msgs, fine):
    shape = jax.ShapeDtypeStruct((FRAMES, fine, 128), jnp.bfloat16)
    return pl.pallas_call(
        rims_kernel,
        out_shape=[shape] * 2,
        in_specs=[VMEM] * FRAMES,
        out_specs=[VMEM] * 2,
        compiler_params=pltpu.CompilerParams(vmem_limit_bytes=3 << 20),
        cost_estimate=pl.CostEstimate(flops=0, bytes_accessed=1_000, transcendentals=0),
    )(*msgs)


def product_kernel(steps, aliased, *refs):
    count = CS * len(steps)
    pieces = refs[:count]
    left2, left1, left0 = refs[count : count + 3]
    skip = count + 3 + (FRAMES if aliased else 0)
    outs = refs[skip : skip + FRAMES]
    weights, acc, sems = refs[skip + FRAMES :]
    y, c = lax.axis_index("y"), lax.axis_index("c")
    cells = outs[0].shape[1]
    copies = []
    for index, step in enumerate(steps):
        for side in range(CS):
            core = c if side == 0 else 1 - c
            piece = pieces[index * CS + side]
            for z in range(ZS):
                source_z = z + core * (ZS - 1 - 2 * z)
                row = pl.multiple_of(index * 128 + source_z * (CS * 8) + core * 8, 8)
                copies.append(
                    pltpu.make_async_copy(
                        piece.at[z, 0:PLANES],
                        weights.at[:, pl.ds(row, 8), :],
                        sems.at[len(copies)],
                    )
                )
    for copy in copies:
        copy.start()
    for copy in copies:
        copy.wait()
    for tap, left in ((2, left2), (1, left1), (0, left0)):
        right = jnp.concatenate([weights[tap * TAPS + t] for t in range(TAPS)], axis=1)
        total = None
        for half in range(2):
            part = lax.dot_general(
                left[half], right, (((1,), (1,)), ((), ())), preferred_element_type=jnp.float32
            )
            total = part if total is None else total + part
        if tap == 2:
            acc[...] = total
        else:
            acc[0 : total.shape[0]] += total
    place = lax.axis_index("x")
    for index, step in enumerate(steps):
        source_y = lax.rem(y + YS - step, YS)
        lanes = slice(index * 128, index * 128 + 128)
        for k, out in enumerate(outs):
            frame = lax.rem(place + FRAMES - k, FRAMES)
            out[source_y] = acc[pl.ds(pl.multiple_of(frame * cells, 8), cells), lanes]


def product(pieces, steps, lefts, before):
    cells = lefts[0].shape[1] // FRAMES
    aliased = before is not None
    inputs = [*pieces, *lefts, *(before if aliased else [])]
    return pl.pallas_call(
        functools.partial(product_kernel, steps, aliased),
        out_shape=[jax.ShapeDtypeStruct((YS, cells, 128), jnp.float32)] * FRAMES,
        in_specs=[pl.BlockSpec(memory_space=pl.ANY)] * len(pieces)
        + [VMEM] * (len(inputs) - len(pieces)),
        out_specs=[VMEM] * FRAMES,
        scratch_shapes=[
            pltpu.VMEM((PLANES, len(steps) * 128, 128), jnp.bfloat16),
            pltpu.VMEM((FRAMES * cells, len(steps) * 128), jnp.float32),
            pltpu.SemaphoreType.DMA((CS * ZS * len(steps),)),
        ],
        input_output_aliases={len(pieces) + 3 + k: k for k in range(FRAMES)} if aliased else {},
        compiler_params=pltpu.CompilerParams(vmem_limit_bytes=12 << 20),
        cost_estimate=pl.CostEstimate(
            flops=1_700_000_000, bytes_accessed=9_000_000, transcendentals=0
        ),
    )(*inputs)


def slope(features, chan, lanes):
    mean, inv, gain, bias = (chan[r : r + 1, lanes] for r in range(4))
    normed = (features.astype(jnp.float32) - mean) * inv
    pre = normed * gain + bias
    sigmoid_pre = 1.0 / (1.0 + jnp.exp(-pre))
    return normed, sigmoid_pre * (1.0 + pre * (1.0 - sigmoid_pre))


def sums_kernel(part0, part1, part2, part3, msg0, msg1, msg2, msg3, chan, kept):
    cells = part0.shape[1]
    for q in range(4):
        lanes = slice(q * 128, q * 128 + 128)
        first = jnp.zeros((8, 128), jnp.float32)
        second = jnp.zeros((8, 128), jnp.float32)
        for part, msg in ((part0, msg0), (part1, msg1), (part2, msg2), (part3, msg3)):
            start = q * cells
            normed, gate = slope(msg[start : start + cells], chan, lanes)
            act = part[q] * gate
            first = first + act.reshape(cells // 8, 8, 128).sum(axis=0)
            second = second + (act * normed).reshape(cells // 8, 8, 128).sum(axis=0)
        kept[q : q + 1] = jnp.sum(first, axis=0, keepdims=True)
        kept[4 + q : 5 + q] = jnp.sum(second, axis=0, keepdims=True)


def partial_sums(parts, msgs, chan):
    return pl.pallas_call(
        sums_kernel,
        out_shape=jax.ShapeDtypeStruct((8, 128), jnp.float32),
        in_specs=[VMEM] * 9,
        out_specs=VMEM,
        compiler_params=pltpu.CompilerParams(vmem_limit_bytes=4 << 20),
        cost_estimate=pl.CostEstimate(
            flops=6_000_000, bytes_accessed=2_900_000, transcendentals=330_000
        ),
    )(*parts, *msgs, chan)


def final_kernel(count, sum0, sum1, sum2, sum3, part0, part1, part2, part3, lat, chan, grad, gain_grad, bias_grad):
    cells, channels = lat.shape
    per_group = channels // GROUPS
    total = (sum0[...] + sum1[...] + (sum2[...] + sum3[...])) / count
    for q in range(4):
        bias_grad[q * 128 : q * 128 + 128] = total[q]
        gain_grad[q * 128 : q * 128 + 128] = total[4 + q]
    row = lax.broadcasted_iota(jnp.int32, (128, 128), 0) // per_group
    col = lax.broadcasted_iota(jnp.int32, (128, 128), 1) // per_group
    same = jnp.where(row == col, 1.0, 0.0)
    gains = jnp.concatenate([chan[2:3, q * 128 : q * 128 + 128] for q in range(4)] * 2, axis=0)
    means = lax.dot_general(
        total * gains,
        same,
        (((1,), (0,)), ((), ())),
        precision=lax.Precision.HIGHEST,
        preferred_element_type=jnp.float32,
    ) / per_group
    for q in range(channels // 128):
        lanes = slice(q * 128, q * 128 + 128)
        normed, gate = slope(lat[:, lanes], chan, lanes)
        up_grad = part0[q] + part1[q] + (part2[q] + part3[q])
        grad[:, lanes] = chan[1:2, lanes] * (
            up_grad * gate * chan[2:3, lanes]
            - means[q : q + 1]
            - normed * means[4 + q : 5 + q]
        )


def final(count, sums, parts, lat, chan):
    return pl.pallas_call(
        functools.partial(final_kernel, count),
        out_shape=[
            jax.ShapeDtypeStruct(lat.shape, jnp.float32),
            jax.ShapeDtypeStruct((lat.shape[1],), jnp.float32),
            jax.ShapeDtypeStruct((lat.shape[1],), jnp.float32),
        ],
        in_specs=[VMEM] * 10,
        out_specs=[VMEM] * 3,
        compiler_params=pltpu.CompilerParams(vmem_limit_bytes=4 << 20),
        cost_estimate=pl.CostEstimate(
            flops=2_000_000, bytes_accessed=1_900_000, transcendentals=82_000
        ),
    )(*sums, *parts, lat, chan)


def on_device(latent, norm_gain, norm_bias, conv_weight, cotangent):
    cells, channels = latent.shape[2], latent.shape[3]
    per_group = channels // GROUPS
    cell_count = FRAMES * ROWS * cells
    own = latent[0, 0]

    block = lax.all_to_all(
        message(latent, conv_weight.reshape(PLANES, 8, 128)),
        ("z", "c"),
        0,
        0,
        axis_index_groups=[
            [z * CS for z in range(ZS)],
            [z * CS + 1 for z in reversed(range(ZS))],
        ],
        tiled=True,
    )

    msgs = [
        msg if step == 0 else send(msg, "x", step)
        for step, msg in enumerate(split(cotangent))
    ]
    pieces = [block] + [send(block, "y", step) for step in range(1, YS)]
    first_rows, last_rows = rims(msgs, cotangent.shape[2])
    pairs = [(i, i + 1) for i in range(1, ROWS - 1, CS)]
    cross = lax.ppermute(first_rows, ROW_AXES, pairs + [(j, i) for i, j in pairs])
    inner = send(last_rows, "c", 1)
    lefts = pool(msgs, cross, inner)
    others = [send(piece, "c", 1) for piece in pieces]
    partial = None
    for steps in ((0, 3), (2, 1)):
        chosen = [piece for step in steps for piece in (pieces[step], others[step])]
        partial = product(chosen, steps, lefts, partial)

    gathered = sum(
        jnp.sum(piece[:, PLANES:].astype(jnp.float32), axis=(0, 1)) for piece in pieces + others
    )
    shared = share(gathered, own)
    lats = [shared] + [send(shared, "x", step) for step in range(1, FRAMES)]
    total = sum(
        lat[first : first + 8].astype(jnp.float32)
        for lat in lats
        for first in range(4 * cells, 4 * cells + 48, 16)
    )
    group = total.reshape(2, GROUPS, per_group).sum(axis=2) / (cell_count * per_group)
    group_mean = group[0]
    group_var = group[1] - group_mean * group_mean
    inv_std = lax.rsqrt(group_var + 1e-06)
    chan = jnp.stack(
        [jnp.repeat(group_mean, per_group), jnp.repeat(inv_std, per_group), norm_gain, norm_bias]
    )

    sums = partial_sums(partial, lats, chan)
    parts = [partial[0]] + [send(partial[FRAMES - step], "x", step) for step in range(1, FRAMES)]
    sums = sums + send(sums, "c", 1)
    sums = jnp.broadcast_to(sums[None], (YS * ZS, 8, 128))
    sums = lax.all_to_all(
        sums,
        ROW_AXES,
        0,
        0,
        axis_index_groups=[list(range(0, ROWS, CS)), list(range(ROWS - 1, 0, -CS))],
        tiled=True,
    ).sum(axis=0)
    sums = [sums] + [send(sums, "x", step) for step in range(1, FRAMES)]
    latent_grad, gain_grad, bias_grad = final(cell_count, sums, parts, own, chan)
    return (latent_grad.reshape(1, 1, cells, channels), gain_grad, bias_grad)


def solution(mesh):
    fine = Mesh(mesh.devices.reshape(XS, YS, ZS, CS), ("x", "y", "z", "c"))
    image = P("x", ROW_AXES, None, None)
    return jax.shard_map(
        on_device,
        mesh=fine,
        in_specs=(image, P(), P(), P(None, None, None, ROW_AXES, "x"), image),
        out_specs=(image, P(), P()),
        check_vma=False,
    )
```
